128 devices in a mesh: gran: 32 (over x, z, core), band: 4 (over y).
Axes of the slice: x: 4, y: 4, z: 4, core: 2. Of those that a mesh axis runs over, the one named last changes fastest.
Arguments:
- prior_grids: float32 [512, 12, 2, 4096], P('gran', 'band'), may hold values from -1.5 to 1.5
- pif_rhs: float32 [512, 12, 2, 4096], P('gran', 'band'), may hold values from -8 to 8
- pif_diagonal: float32 [512, 12, 2, 4096], P('gran', 'band'), may hold values from 0.5 to 2
- pif_cross: float32 [512, 12, 4096], P('gran', 'band'), may hold values from -0.7 to 0.7
- pif_coupling: bfloat16 [512, 8, 12, 4096], P('gran', None, 'band'), may hold values from 0.25 to 2
- neighbour_offset: int32 [512, 8], P('gran'), may hold values from -4 to 4, as said below
- neighbour_count: int32 [512], P('gran'), may hold values from 1 to 8, as said below
- tile_route: int32 [512, 2], replicated, may hold values from 0 to 31, all different within a row; in each aligned block of 16 rows (0 to 15, 16 to 31, ...) at most 2 rows name the same one
- tile_window: int32 [512, 2, 2], replicated, may hold values from 0 to 1760
- tile_pixels: bfloat16 [32, 12, 256, 256], P('gran', 'band'), may hold values from 0.049804688 to 1
Outputs:
- balanced_grids: float32 [512, 12, 2, 4096], P('gran', 'band')
- corrected_tiles: bfloat16 [32, 12, 256, 256], P('gran', 'band')
The draws below stay inside these ranges and needn't reach their ends.
Inputs may be any that keep to these rules, and one draw needn't show every extreme that they name: `neighbour_offset`: A granule's slots below its count hold a nonzero offset to another granule; the other slots hold 0. In every aligned block of 16 granules the granule of count 8 has an offset of magnitude 4 in its first slot. `neighbour_count`: every aligned block of 16 granules holds a granule with 8 neighbours. `tile_route`: each granule names two different tiles; every tile is named; among the 16 granules of one device no tile is named more than 2 times.
All inputs are finite; a program needn't handle non-finite values.
Results may differ from the reference program's by a relative error of at most 0.0036.
The reference program's roundings to bfloat16 on the way count: a program that leaves them out, or rounds other values in their place, can miss the bound.
Values may be sent and summed in bfloat16 or wider, within the bound.
A program may use at most 128 MiB of HBM per device.

```python
import math
import jax
import jax.numpy as jnp
import numpy as np
from jax import lax

BANDS = 12
KN = 64
KNOTS = 4096
PATCH = 8
DEG = 8
REACH = 4
SWEEPS = 3
SP = 32
PIX = 256
G_DEV = 16
GRANULES = 512
TILES = 32
MOST = 2


def neighbour_graph(key):
    key = jax.random.fold_in(key, 7301)
    key_degree, key_hub, key_reach, key_sign = jax.random.split(key, 4)
    granule_index = jnp.arange(GRANULES, dtype=jnp.int32)
    block_total = GRANULES // G_DEV
    degrees = jax.random.randint(key_degree, (GRANULES,), 1, 4, dtype=jnp.int32)
    hub_place = jax.random.randint(key_hub, (block_total,), 0, G_DEV, dtype=jnp.int32)
    is_hub = granule_index % G_DEV == jnp.repeat(hub_place, G_DEV)
    degrees = jnp.where(is_hub, DEG, degrees)
    slot_index = jnp.arange(DEG, dtype=jnp.int32)[None, :]
    reach_size = jax.random.randint(key_reach, (GRANULES, DEG), 1, REACH + 1, dtype=jnp.int32)
    reach_size = jnp.where(is_hub[:, None] & (slot_index == 0), REACH, reach_size)
    direction = jax.random.randint(key_sign, (GRANULES, DEG), 0, 2, dtype=jnp.int32) * 2 - 1
    offsets = reach_size * direction
    target = granule_index[:, None] + offsets
    offsets = jnp.where((target < 0) | (target >= GRANULES), -offsets, offsets)
    offsets = jnp.where(slot_index < degrees[:, None], offsets, 0)
    return (offsets, degrees)


def draw_neighbour_offset(key, part):
    return neighbour_graph(key)[0]


def draw_neighbour_count(key, part):
    return neighbour_graph(key)[1]


def draw_pif_rhs(key, part):
    key_base = jax.random.fold_in(jax.random.fold_in(key, 911), 0)
    band_scale = 0.6 * 3.0 ** (jnp.arange(BANDS, dtype=jnp.float32) / (BANDS - 1))
    shape_all = (GRANULES, BANDS, 2, KNOTS)
    base_value = jnp.clip(jax.random.normal(key_base, shape_all, jnp.float32), -4.0, 4.0)
    return base_value * band_scale[None, :, None, None]


def set_ends(array, own_key, low, top_value):
    longest = array.shape.index(max(array.shape))
    spots = []
    for shift in (0, 1):
        where = [jax.random.randint(jax.random.fold_in(own_key, axis), (), 0, length) for axis, length in enumerate(array.shape)]
        where[longest] = (where[longest] + shift) % array.shape[longest]
        spots.append(tuple(where))
    return array.at[spots[0]].set(low).at[spots[1]].set(top_value)


def steps_of(stream_key, dims, cuts, least, largest):
    def one(axis_at, blocks):
        draws = jax.random.uniform(jax.random.fold_in(jax.random.fold_in(stream_key, 6), axis_at), (blocks,), jnp.float32, least / len(cuts), largest / len(cuts))
        return jnp.repeat(jnp.exp(draws), dims[axis_at] // blocks).reshape((-1,) + (1,) * (len(dims) - axis_at - 1))

    factor_of = one(*cuts[0])
    for cut in cuts[1:]:
        factor_of = factor_of * one(*cut)
    return factor_of


def assign_block(key, own, number, rows, count, top, bound, lean):
    sequence = jax.random.permutation(key, count)
    crowded, ordinary = load_shares(count, rows * top, bound, lean, True), load_shares(count, rows * top, bound, lean, False)
    places = jnp.arange(count)

    def named(sizes, offset_by):
        used = int((sizes > 0).sum())
        fixed = max(1, used // 4)
        passed = fixed + (places - fixed + offset_by * (used - fixed)) % max(1, count - fixed)
        return jnp.zeros((count,), jnp.int32).at[sequence[jnp.where(places < fixed, places, passed)]].set(jnp.asarray(sizes, jnp.int32))

    sizes = jnp.where(number % 4 == 0, named(crowded, number // 4), named(ordinary, number - number // 4 - 1))
    mixed = jax.random.permutation(jax.random.fold_in(own, 3), count)
    donor, taker = mixed[0:count // 2 * 2:2], mixed[1:count // 2 * 2:2]
    room = jnp.minimum(sizes[donor] - 1, bound - sizes[taker]) // 2
    room = jnp.where((donor == sequence[0]) | (taker == sequence[0]) | (sizes[taker] == 0), 0, jnp.maximum(room, 0))
    passed = jax.random.randint(jax.random.fold_in(own, 4), (count // 2,), 0, 1 << 20) % (room + 1)
    sizes = sizes.at[donor].add(-passed).at[taker].add(passed)
    items = jnp.searchsorted(jnp.cumsum(sizes), jnp.arange(rows * top), side="right").astype(jnp.int32)
    listing = items.reshape(top, rows).T
    listing = listing[jax.random.permutation(jax.random.fold_in(own, 1), rows)]
    offset_by = jax.random.randint(jax.random.fold_in(own, 2), (rows, 1), 0, top)
    return jnp.take_along_axis(listing, (jnp.arange(top)[None, :] + offset_by) % top, axis=1)


def load_shares(amount, total, reach, slope, full):
    weights = [(1 << 20) // math.isqrt(standing ** slope) + 1 for standing in range(1, amount + 1)]
    largest = reach if full else min(reach, max(-(-total // amount), total * weights[0] // sum(weights)))
    least = 1 if total - largest >= amount - 1 else 0
    counts, rest = [largest] + [least] * (amount - 1), total - largest - least * (amount - 1)
    while rest > 0:
        movable = [i for i in range(1, amount) if counts[i] < largest] or [i for i in range(1, amount) if counts[i] < reach]
        mass, remaining = sum([weights[i] for i in movable]), rest
        for i in movable:
            extra = min(reach - counts[i], max(1, remaining * weights[i] // mass), rest)
            counts[i] = counts[i] + extra
            rest = rest - extra
    return np.array(counts)


def bell_draw(stream_key, dims, deviation, reach, cuts=(), held_as=jnp.bfloat16):
    array = deviation * jax.random.normal(stream_key, dims, jnp.float32)
    if cuts:
        array = array * steps_of(stream_key, dims, cuts, -0.22, 0.18)
    return jnp.clip(array, -reach, reach).astype(held_as)


def setup_inputs(seed: int = 0) -> dict:
    arg_keys = jax.random.split(jax.random.key(seed), 11)
    prior_grids = bell_draw(arg_keys[0], (GRANULES, BANDS, 2, KNOTS), 0.3, 1.5, ((0, 32), (1, 4)), jnp.float32)
    pif_rhs = draw_pif_rhs(jax.random.fold_in(arg_keys[10], 71), 0)
    pif_diagonal = jnp.clip(jnp.exp(math.log(2.0) - 1.3862944 * jax.random.uniform(arg_keys[2], (GRANULES, BANDS, 2, KNOTS), jnp.float32) ** steps_of(arg_keys[2], (GRANULES, BANDS, 2, KNOTS), ((0, 32), (1, 4)), -0.2, 0.2)), 0.5, 2.0)
    pif_cross = jnp.clip(jax.random.uniform(arg_keys[3], (GRANULES, BANDS, KNOTS), jnp.float32, -0.7, 0.7) * steps_of(arg_keys[3], (GRANULES, BANDS, KNOTS), ((0, 32), (1, 4)), -0.4, 0.0), -0.7, 0.7)
    pif_coupling = jnp.clip(jnp.exp(math.log(2.0) - 2.0794415 * jax.random.uniform(arg_keys[4], (GRANULES, DEG, BANDS, KNOTS), jnp.float32) ** steps_of(arg_keys[4], (GRANULES, DEG, BANDS, KNOTS), ((0, 32), (2, 4)), -0.2, 0.2)), 0.25, 2.0).astype(jnp.bfloat16)
    neighbour_offset = draw_neighbour_offset(jax.random.fold_in(arg_keys[10], 71), 0)
    neighbour_count = draw_neighbour_count(jax.random.fold_in(arg_keys[10], 71), 0)
    tile_route_keys = jax.random.split(jax.random.fold_in(arg_keys[7], 1), GRANULES // G_DEV)
    tile_route_turns = jax.random.permutation(jax.random.fold_in(arg_keys[7], 3), GRANULES // G_DEV)
    tile_route = jax.vmap(lambda own, number: assign_block(jax.random.fold_in(arg_keys[7], 2), own, number, G_DEV, TILES, 2, MOST, 2))(tile_route_keys, tile_route_turns).reshape((GRANULES, 2))
    tile_window = set_ends(jax.random.randint(arg_keys[8], (GRANULES, 2, 2), 0, (KN - 1) * SP - PIX + 1), jax.random.fold_in(arg_keys[8], 1), 0, (KN - 1) * SP - PIX).astype(jnp.int32)
    tile_pixels = jnp.clip(jnp.exp(math.log(1.0) - 2.9996462 * jax.random.uniform(arg_keys[9], (TILES, BANDS, PIX, PIX), jnp.float32) ** steps_of(arg_keys[9], (TILES, BANDS, PIX, PIX), ((0, 32), (1, 4)), -0.2, 0.2)), 0.049804688, 1.0).astype(jnp.bfloat16)
    return dict(prior_grids=prior_grids, pif_rhs=pif_rhs, pif_diagonal=pif_diagonal, pif_cross=pif_cross, pif_coupling=pif_coupling, neighbour_offset=neighbour_offset, neighbour_count=neighbour_count, tile_route=tile_route, tile_window=tile_window, tile_pixels=tile_pixels)


cubic_sharpness = -0.5
robust_scale = 0.3

def cubic_taps(fraction):
    sharpness = cubic_sharpness

    def near_tap(distance):
        return (sharpness + 2.0) * distance ** 3 - (sharpness + 3.0) * distance ** 2 + 1.0

    def far_tap(distance):
        return sharpness * distance ** 3 - 5.0 * sharpness * distance ** 2 + 8.0 * sharpness * distance - 4.0 * sharpness
    return (far_tap(1.0 + fraction), near_tap(fraction), near_tap(1.0 - fraction), far_tap(2.0 - fraction))

def interp_matrix(start_pixel, length, first_knot, extent):
    pixel_index = start_pixel + jnp.arange(length, dtype=jnp.int32)
    base_knot = pixel_index // SP
    fraction = (pixel_index - base_knot * SP).astype(jnp.float32) / SP
    columns = jnp.arange(extent, dtype=jnp.int32)
    result = jnp.zeros((length, extent), jnp.float32)
    for shift_value, tap_weight in zip((-1, 0, 1, 2), cubic_taps(fraction)):
        knot_index = jnp.clip(base_knot + shift_value, 0, KN - 1) - first_knot
        result = result + tap_weight[:, None] * (knot_index[:, None] == columns[None, :]).astype(jnp.float32)
    return result.astype(jnp.bfloat16)

def patch_total(values):
    leading = values.shape[:-1]
    blocks = KN // PATCH
    blocked = values.reshape(leading + (blocks, PATCH, blocks, PATCH))
    return lax.optimization_barrier(jnp.sum(blocked, axis=(-3, -1))).reshape(leading + (blocks * blocks,))

def patch_spread(values):
    leading = values.shape[:-1]
    blocks = KN // PATCH
    blocked = values.reshape(leading + (blocks, 1, blocks, 1))
    return jnp.broadcast_to(blocked, leading + (blocks, PATCH, blocks, PATCH)).reshape(leading + (KN * KN,))

def solve_pairs(pif_diagonal, pif_cross, diagonal_add, drive_term):
    gain_pivot = pif_diagonal[:, :, 0] + diagonal_add
    offset_pivot = pif_diagonal[:, :, 1] + diagonal_add
    cross_term = pif_cross * jnp.sqrt(pif_diagonal[:, :, 0] * pif_diagonal[:, :, 1])
    determinant = gain_pivot * offset_pivot - cross_term * cross_term
    gain_part = (offset_pivot * drive_term[:, :, 0] - cross_term * drive_term[:, :, 1]) / determinant
    offset_part = (gain_pivot * drive_term[:, :, 1] - cross_term * drive_term[:, :, 0]) / determinant
    return jnp.stack([gain_part, offset_part], axis=2)

def reference(prior_grids, pif_rhs, pif_diagonal, pif_cross, pif_coupling, neighbour_offset, neighbour_count, tile_route, tile_window, tile_pixels):
    granule_index = jnp.arange(GRANULES, dtype=jnp.int32)
    neighbour = granule_index[:, None] + neighbour_offset
    slot_weight = (jnp.arange(DEG, dtype=jnp.int32)[None, :] < neighbour_count[:, None]).astype(jnp.float32)
    knot_grids = prior_grids
    for sweep_index in range(SWEEPS):
        response = knot_grids[:, :, 0] + knot_grids[:, :, 1]
        diagonal_add = jnp.zeros((GRANULES, BANDS, KNOTS), jnp.float32)
        drive_term = pif_rhs
        for slot_index in range(DEG):
            partner = neighbour[:, slot_index]
            difference = response - response[partner]
            disparity = patch_total(lax.optimization_barrier(jnp.sum(difference * difference, axis=1)))
            robust = slot_weight[:, slot_index, None] / (1.0 + disparity / (robust_scale * BANDS * PATCH * PATCH))
            effective = patch_spread(robust)[:, None, :] * pif_coupling[:, slot_index].astype(jnp.float32)
            diagonal_add = diagonal_add + effective
            drive_term = drive_term + effective[:, :, None, :] * knot_grids[partner]
        knot_grids = solve_pairs(pif_diagonal, pif_cross, diagonal_add, drive_term)
    shaped = knot_grids.astype(jnp.bfloat16).reshape(GRANULES, BANDS, 2, KN, KN)

    def contribute(entry_index, field_sum):
        granule = entry_index // 2
        route_slot = entry_index % 2
        tile_index = tile_route[granule, route_slot]
        row_start = tile_window[granule, route_slot, 0].astype(jnp.int32)
        col_start = tile_window[granule, route_slot, 1].astype(jnp.int32)
        row_weights = interp_matrix(row_start, PIX, 0, KN).astype(jnp.float32)
        col_weights = interp_matrix(col_start, PIX, 0, KN).astype(jnp.float32)
        knot_values = shaped[granule].astype(jnp.float32)
        rowpass = jnp.einsum('pk,bckl->bcpl', row_weights, knot_values, precision=lax.Precision.HIGHEST)
        rowpass = lax.optimization_barrier(rowpass.astype(jnp.bfloat16)).astype(jnp.float32)
        contribution = jnp.einsum('bcpl,ql->bcpq', rowpass, col_weights, precision=lax.Precision.HIGHEST)
        return field_sum.at[tile_index].add(contribution)
    field_sum = lax.fori_loop(0, 2 * GRANULES, contribute, jnp.zeros((TILES, BANDS, 2, PIX, PIX), jnp.float32))
    covers = lax.optimization_barrier(jnp.sum((tile_route.reshape(-1)[:, None] == jnp.arange(TILES, dtype=jnp.int32)[None, :]).astype(jnp.int32), axis=0))
    covers = covers.astype(jnp.float32)[:, None, None, None]
    pixels = tile_pixels.astype(jnp.float32)
    corrected = pixels * (1.0 + field_sum[:, :, 0] / covers) + field_sum[:, :, 1] / covers
    return (knot_grids, corrected.astype(jnp.bfloat16))
```

```python
import jax
import jax.numpy as jnp
from jax import lax
from jax.experimental import pallas as pl
from jax.experimental.pallas import tpu as pltpu
from jax.sharding import PartitionSpec as P

MESH = pl.DeviceIdType.MESH
F32 = jnp.float32
BF16 = jnp.bfloat16
I32 = jnp.int32

BANDS = 12
PATCH = 8
REACH = 4
SWEEPS = 3
SP = 32
ROBUST = 0.3 * BANDS * PATCH * PATCH

GD = 16
BD_ = 3
NG = 32
NB = 4
SLOTS = 8
PIX = 256
WIN = 16
FIRST_MAX = 64 - WIN
FAR = 1000.0


def iota(shape, dim):
    return lax.broadcasted_iota(I32, shape, dim)


def dot(a, b):
    return jnp.dot(a, b, preferred_element_type=F32)


def split_dot(x, table):
    high = x.astype(BF16)
    low = (x - high.astype(F32)).astype(BF16)
    return dot(high, table) + dot(low, table)


def butterfly(x, lane, width, op):
    size = x.shape[1]
    step = 1
    while step < width:
        other = jnp.where(
            (lane // step) % 2 == 0,
            pltpu.roll(x, size - step, axis=1),
            pltpu.roll(x, step, axis=1),
        )
        x = op(x, other)
        step *= 2
    return x


def far_tap(d):
    return ((-0.5 * d + 2.5) * d - 4.0) * d + 2.0


def near_tap(d):
    return (1.5 * d - 2.5) * d * d + 1.0


def edge_granule(k):
    return k + (k // 4) * 8


def inner_granule(k):
    return k + 4


def kernel(
    off_s,
    cnt_s,
    prior_h,
    rhs_h,
    diag_h,
    cross_h,
    coup_h,
    route_v,
    win_v,
    pix_h,
    bal_h,
    tile_h,
    prior_b,
    rhs_b,
    diag_b,
    cross_b,
    coup_b,
    pix_b,
    out_b,
    tile_b,
    grids,
    resp,
    coup,
    cterm,
    disp,
    spread,
    weight,
    halo_out,
    halo_in,
    part_out,
    part_in,
    tab_v,
    tab_s,
    pay_out,
    pay_in,
    roww,
    colw,
    diagonal,
    rowpass,
    in_sem,
    out_sem,
    hs_sem,
    hr_sem,
    ps_sem,
    pr_sem,
    as_sem,
    ar_sem,
    tab_sem,
    own_sem,
):
    me = lax.axis_index("gran")
    mb = lax.axis_index("band")
    right = lax.rem(me + 1, NG)
    left = lax.rem(me + NG - 1, NG)

    loads = [
        pltpu.make_async_copy(src, dst, in_sem.at[n])
        for n, (src, dst) in enumerate(
            (
                (prior_h, prior_b),
                (coup_h, coup_b),
                (cross_h, cross_b),
                (diag_h, diag_b),
                (rhs_h, rhs_b),
                (pix_h, pix_b),
            )
        )
    ]
    for load in loads:
        load.start()

    barrier = pltpu.get_barrier_semaphore()

    def greet_gran(k, carry):
        pl.semaphore_signal(
            barrier, inc=1, device_id=(lax.rem(me + k, NG), mb), device_id_type=MESH
        )
        return carry

    lax.fori_loop(1, NG, greet_gran, 0)
    for k in range(1, NB):
        pl.semaphore_signal(
            barrier, inc=1, device_id=(me, lax.rem(mb + k, NB)), device_id_type=MESH
        )

    lane128 = iota((128, 128), 1)
    sub128 = iota((128, 128), 0)
    gather_table = ((sub128 % 64) // 8 == lane128 % 8).astype(F32).astype(BF16)
    spread_table = ((lane128 % 64) // 8 == sub128 % 8).astype(F32).astype(BF16)
    block32 = iota((32, 128), 1) // 8

    loads[0].wait()

    def take_prior(i, carry):
        for b in range(BD_):
            for v in range(4):
                g0 = prior_b[i, b, pl.ds(2 * v, 8, stride=8), :]
                g1 = prior_b[i, b, pl.ds(2 * v + 1, 8, stride=8), :]
                grids[0, REACH + i, b, 0, v] = g0
                grids[0, REACH + i, b, 1, v] = g1
                resp[REACH + i, b, v] = g0 + g1
        return carry

    lax.fori_loop(0, GD, take_prior, 0)

    def first_halo(k, carry):
        i = edge_granule(k)
        side = 1 - k // 4
        e = lax.rem(k, 4)
        for b in range(BD_):
            halo_out[0, side, 0, e, b] = resp[REACH + i, b].reshape(32, 128).astype(BF16)
            halo_out[0, side, 1, e, b] = grids[0, REACH + i, b, 0].reshape(32, 128).astype(BF16)
        return carry

    lax.fori_loop(0, 8, first_halo, 0)

    pl.semaphore_wait(barrier, NG - 1 + NB - 1)

    def halo_copy(sweep, side, piece):
        return pltpu.make_async_remote_copy(
            src_ref=halo_out.at[sweep, side, piece],
            dst_ref=halo_in.at[sweep, side, piece],
            send_sem=hs_sem.at[sweep, side, piece],
            recv_sem=hr_sem.at[sweep, side, piece],
            device_id=(right if side == 0 else left, mb),
            device_id_type=MESH,
        )

    def start_halo(sweep):
        for piece in range(2):
            for side in range(2):
                halo_copy(sweep, side, piece).start()

    def part_copy(sweep, part, k):
        return pltpu.make_async_remote_copy(
            src_ref=part_out.at[sweep, part],
            dst_ref=part_in.at[sweep, part, k - 1],
            send_sem=ps_sem.at[sweep, part, k - 1],
            recv_sem=pr_sem.at[sweep, part, k - 1],
            device_id=(me, lax.rem(mb + k, NB)),
            device_id_type=MESH,
        )

    start_halo(0)

    slot = (iota((32, 128), 1) // 64) * 4 + iota((32, 128), 0) // 8
    for part, granule_of in ((0, inner_granule), (1, edge_granule)):
        counts = jnp.zeros((32, 128), I32)
        for k in range(8):
            counts = jnp.where(block32 % 8 == k, cnt_s[granule_of(k)], counts)
        weight[part] = (slot < counts).astype(F32)

    def disparity(part, sweep):
        granule_of = (inner_granule, edge_granule)[part]

        def one(k, carry):
            i = granule_of(k)
            own = [resp[REACH + i, b] for b in range(BD_)]
            for s in range(SLOTS):
                n = REACH + i + off_s[s, i]
                total = None
                for b in range(BD_):
                    diff = own[b] - resp[n, b]
                    square = diff * diff
                    total = square if total is None else total + square
                disp[pl.ds(pl.multiple_of(k * 64 + s * 8, 8), 8), :] = (
                    total[0] + total[1] + total[2] + total[3]
                )
            return carry

        lax.fori_loop(0, 8, one, 0)
        sums = split_dot(disp[...], gather_table)
        packed = jnp.zeros((32, 128), F32)
        for k in range(8):
            for h in range(2):
                rows = sums[k * 64 + h * 32 : k * 64 + h * 32 + 32]
                packed = jnp.where(block32 == h * 8 + k, rows, packed)
        part_out[sweep, part] = packed
        for k in (2, 1, 3):
            part_copy(sweep, part, k).start()

    def solve(part, sweep):
        granule_of = (inner_granule, edge_granule)[part]
        now, later = sweep % 2, (sweep + 1) % 2
        last = sweep == SWEEPS - 1
        for k in range(1, NB):
            part_copy(sweep, part, k).wait_recv()
        total = part_out[sweep, part]
        for k in range(NB - 1):
            total = total + part_in[sweep, part, k]
        robust = weight[part] / (1.0 + total * (1.0 / ROBUST))
        rows = []
        for k in range(8):
            for h in range(2):
                rows.append(jnp.where(block32 == h * 8 + k, robust, 0.0))
        spread[...] = split_dot(jnp.concatenate(rows, axis=0), spread_table)

        def one(k, carry):
            i = granule_of(k)
            places = [REACH + i + off_s[s, i] for s in range(SLOTS)]
            for b in range(BD_):
                sigma = drive0 = drive1 = None
                for s in range(SLOTS):
                    rob = spread[pl.ds(pl.multiple_of(k * 64 + s * 8, 8), 8), :]
                    eff = rob[None] * coup[i, b, s]
                    add0 = eff * grids[now, places[s], b, 0]
                    add1 = eff * grids[now, places[s], b, 1]
                    if s == 0:
                        sigma, drive0, drive1 = eff, add0, add1
                    else:
                        sigma, drive0, drive1 = sigma + eff, drive0 + add0, drive1 + add1
                for v in range(4):
                    even = pl.ds(2 * v, 8, stride=8)
                    odd = pl.ds(2 * v + 1, 8, stride=8)
                    r0 = rhs_b[i, b, even, :] + drive0[v]
                    r1 = rhs_b[i, b, odd, :] + drive1[v]
                    first = diag_b[i, b, even, :] + sigma[v]
                    second = diag_b[i, b, odd, :] + sigma[v]
                    cross = cterm[i, b, v]
                    inverse = 1.0 / (first * second - cross * cross)
                    g0 = (second * r0 - cross * r1) * inverse
                    g1 = (first * r1 - cross * r0) * inverse
                    if last:
                        out_b[i, b, even, :] = g0
                        out_b[i, b, odd, :] = g1
                    else:
                        grids[later, REACH + i, b, 0, v] = g0
                        grids[later, REACH + i, b, 1, v] = g1
                        resp[REACH + i, b, v] = g0 + g1
                if part == 1 and not last:
                    side = 1 - k // 4
                    e = lax.rem(k, 4)
                    halo_out[sweep + 1, side, 0, e, b] = (
                        resp[REACH + i, b].reshape(32, 128).astype(BF16)
                    )
                    halo_out[sweep + 1, side, 1, e, b] = (
                        grids[later, REACH + i, b, 0].reshape(32, 128).astype(BF16)
                    )
            return carry

        lax.fori_loop(0, 8, one, 0)
        if part == 1 and not last:
            start_halo(sweep + 1)

    def take_responses(sweep):
        for side in range(2):
            halo_copy(sweep, side, 0).wait_recv()

            def one(e, carry, side=side):
                for b in range(BD_):
                    value = halo_in[sweep, side, 0, e, b].astype(F32)
                    resp[e + side * (REACH + GD), b] = value.reshape(4, 8, 128)
                return carry

            lax.fori_loop(0, REACH, one, 0)

    def take_grids(sweep):
        now = sweep % 2
        for side in range(2):
            halo_copy(sweep, side, 1).wait_recv()

            def one(e, carry, side=side):
                place = e + side * (REACH + GD)
                for b in range(BD_):
                    g0 = halo_in[sweep, side, 1, e, b].astype(F32).reshape(4, 8, 128)
                    grids[now, place, b, 0] = g0
                    grids[now, place, b, 1] = resp[place, b] - g0
                return carry

            lax.fori_loop(0, REACH, one, 0)

    def take_coupling():
        row = iota((256, 256), 0)
        source = (4 * (row % 8) + (row // 8) % 4) * 8 + row // 32
        order = (iota((256, 256), 1) == source).astype(F32).astype(BF16)

        def one(i, carry):
            for b in range(BD_):
                coup[i, b] = dot(order, coup_b[i, b]).reshape(8, 4, 8, 128)
            return carry

        lax.fori_loop(0, GD, one, 0)

    def take_cross():
        def one(half, carry):
            for g in range(8):
                i = half * 8 + g
                for b in range(BD_):
                    for v in range(4):
                        d0 = diag_b[i, b, pl.ds(2 * v, 8, stride=8), :]
                        d1 = diag_b[i, b, pl.ds(2 * v + 1, 8, stride=8), :]
                        value = cross_b[b, half, pl.ds(8 * v + g, 8, stride=32), :]
                        cterm[i, b, v] = value * jnp.sqrt(d0 * d1)
            return carry

        lax.fori_loop(0, 2, one, 0)

    def send_table():
        block = pl.multiple_of((me // 8) * 128, 128)
        turn = lax.rem(128 - lax.rem(me, 8) * 16, 128)
        lane = iota((32, 128), 1)
        tile = iota((32, 128), 0)

        def own(ref_rows):
            pair = []
            for route in range(2):
                row = jnp.broadcast_to(ref_rows(route, pl.ds(block, 128)), (32, 128))
                row = pltpu.roll(row, turn, axis=1)
                pair.append(pltpu.roll(row, 16, axis=1) if route else row)
            return jnp.where(lane < 16, pair[0], pair[1])

        routes = own(lambda route, cols: route_v[pl.ds(route, 1), cols])
        starts = [
            own(lambda route, cols, c=c: win_v[route, pl.ds(c, 1), cols]) for c in range(2)
        ]
        match = (routes == tile) & (lane < 32)
        low = butterfly(jnp.where(match, lane, 99), lane, 32, jnp.minimum)
        high = butterfly(jnp.where(match, lane, -1), lane, 32, jnp.maximum)
        table = jnp.zeros((32, 128), I32)
        for rank, chosen in enumerate((low, high)):
            picks = [
                butterfly(
                    jnp.where((lane == chosen) & (lane < 32), start, 0), lane, 32, jnp.add
                )
                for start in starts
            ]
            valid = (chosen >= 0) & (chosen < 32)
            granule = jnp.where(valid, chosen % 16, 0)
            first = [jnp.clip(pick // SP - 1, 0, FIRST_MAX) for pick in picks]
            for column, value in enumerate((granule, first[0] // 2, first[1])):
                table = jnp.where(lane == rank * 3 + column, value, table)
        tab_v[...] = table
        copy = pltpu.make_async_copy(tab_v, tab_s, tab_sem)
        copy.start()
        copy.wait()

    def weights():
        lane = iota((8, 512), 1)
        place = lane % 16
        match = []
        for route in range(2):
            row = jnp.broadcast_to(route_v[pl.ds(route, 1), :], (8, 512))
            match.append(row == me)
        low = jnp.minimum(
            jnp.where(match[0], place, 99), jnp.where(match[1], place + 16, 99)
        )
        high = jnp.maximum(
            jnp.where(match[0], place, -1), jnp.where(match[1], place + 16, -1)
        )
        low = butterfly(low, lane, 16, jnp.minimum)
        high = butterfly(high, lane, 16, jnp.maximum)
        total = jnp.sum(
            (match[0].astype(F32) + match[1].astype(F32))[0:1], axis=1, keepdims=True
        )
        for rank, chosen in enumerate((low, high)):
            live = (chosen < 32) if rank == 0 else (high != low) & (chosen >= 0)
            for coord, ref in enumerate((roww, colw)):
                pick = jnp.zeros((8, 512), I32)
                for route in range(2):
                    row = jnp.broadcast_to(win_v[route, pl.ds(coord, 1), :], (8, 512))
                    pick = pick + jnp.where(chosen == place + 16 * route, row, 0)
                pick = butterfly(pick, lane, 16, jnp.add)
                first = jnp.clip(pick // SP - 1, 0, FIRST_MAX)
                if coord == 0:
                    knot = (first // 2) * 2 + 2 * (place % 8) + place // 8
                else:
                    knot = first + place
                knot_f = knot.astype(F32)
                extra = jnp.where(
                    knot == 0, -1.0, jnp.where(knot == 63, 64.0, FAR)
                )
                start = pick.astype(F32) * (1.0 / SP)
                lead = start - knot_f
                lead_extra = start - extra

                def rows(block, carry, ref=ref, rank=rank, lead=lead, lead_extra=lead_extra,
                         live=live, coord=coord):
                    parts = []
                    for h in range(2):
                        pixel = (
                            iota((8, 512), 0) + (block * 16 + h * 8)
                        ).astype(F32) * (1.0 / SP)
                        d = jnp.abs(lead + pixel)
                        w = jnp.where(d <= 1.0, near_tap(d), far_tap(d))
                        w = jnp.where(d < 2.0, w, 0.0)
                        d2 = jnp.abs(lead_extra + pixel)
                        w = w + jnp.where(d2 < 2.0, far_tap(d2), 0.0)
                        if coord == 1:
                            w = jnp.where(live, w, 0.0)
                        parts.append(w)
                    ref[pl.ds(pl.multiple_of(block * 16, 16), 16), rank * 512 : rank * 512 + 512] = (
                        jnp.concatenate(parts, axis=0).astype(BF16)
                    )
                    return carry

                lax.fori_loop(0, PIX // 16, rows, 0)
        return 1.0 / total

    def clear_diagonal():
        def one(n, carry):
            diagonal[n] = jnp.zeros((256, 256), BF16)
            return carry

        lax.fori_loop(0, 24, one, 0)

    disparity(0, 0)
    loads[1].wait()
    take_coupling()
    take_responses(0)
    disparity(1, 0)
    loads[2].wait()
    loads[3].wait()
    take_cross()
    take_grids(0)
    loads[4].wait()
    solve(0, 0)
    solve(1, 0)

    disparity(0, 1)
    send_table()
    inverse_cover = weights()
    take_responses(1)
    disparity(1, 1)
    take_grids(1)
    solve(0, 1)
    solve(1, 1)

    disparity(0, 2)
    clear_diagonal()
    take_responses(2)
    disparity(1, 2)
    take_grids(2)
    solve(0, 2)
    solve(1, 2)

    save = pltpu.make_async_copy(out_b, bal_h, out_sem.at[0])
    save.start()

    lane8 = iota((8, 128), 1)
    lane_band = (lane8 % 64) // 16

    def fill(t, carry):
        for rank in range(2):
            granule = tab_s[t, rank * 3]
            row = tab_s[t, rank * 3 + 1]
            column = tab_s[t, rank * 3 + 2]
            halves = []
            for c in range(2):
                value = None
                for b in range(BD_):
                    x = out_b[granule, b, pl.ds(2 * row + c, 8, stride=2), :]
                    x = pltpu.roll(x, lax.rem(b * 16 + 128 - column, 128), axis=1)
                    value = x if value is None else jnp.where(lane_band == b, x, value)
                halves.append(value)
            pay_out[t, rank * 16 : rank * 16 + 16, :] = jnp.concatenate(halves, axis=0).astype(BF16)
        return carry

    lax.fori_loop(0, NG, fill, 0)

    def pay_copy(k):
        return pltpu.make_async_remote_copy(
            src_ref=pay_out.at[lax.rem(me + k, NG)],
            dst_ref=pay_in.at[me],
            send_sem=as_sem.at[k],
            recv_sem=ar_sem.at[k],
            device_id=(lax.rem(me + k, NG), mb),
            device_id_type=MESH,
        )

    def send_pay(k, carry):
        pay_copy(k).start()
        return carry

    lax.fori_loop(1, NG, send_pay, 0)
    own_copy = pltpu.make_async_copy(pay_out.at[me], pay_in.at[me], own_sem)
    own_copy.start()
    loads[5].wait()
    own_copy.wait()

    def take_pay(k, carry):
        pltpu.make_async_remote_copy(
            src_ref=pay_out.at[lax.rem(me + k, NG)],
            dst_ref=pay_in.at[lax.rem(me + NG - k, NG)],
            send_sem=as_sem.at[k],
            recv_sem=ar_sem.at[k],
            device_id=(lax.rem(me + k, NG), mb),
            device_id_type=MESH,
        ).wait_recv()
        return carry

    lax.fori_loop(1, NG, take_pay, 0)

    def expand(group, carry):
        rank = group // 2
        base = lax.rem(group, 2) * 16
        for s in range(16):
            block = pay_in[base + s, pl.ds(pl.multiple_of(rank * 16, 16), 16), :].astype(F32)
            for c in range(2):
                x = block[c * 8 : c * 8 + 8]
                for b in range(BD_):
                    parts = []
                    for parity in range(2):
                        turn = ((s % 8) * 16 - parity * 64 - b * 16) % 128
                        y = pltpu.roll(x, turn, axis=1) if turn else x
                        parts.append(jnp.where(lane8 // 16 == s % 8, y, 0.0))
                    diagonal[
                        group * 6 + b * 2 + c,
                        s * 16 : s * 16 + 16,
                        (s // 8) * 128 : (s // 8) * 128 + 128,
                    ] = jnp.concatenate(parts, axis=0).astype(BF16)
        return carry

    lax.fori_loop(0, 4, expand, 0)

    def correct(b, carry):
        fields = []
        for c in range(2):
            for group in range(4):
                cols = slice(group * 256, group * 256 + 256)
                rowpass[:, cols] = dot(roww[:, cols], diagonal[group * 6 + b * 2 + c]).astype(BF16)
            fields.append(
                lax.dot_general(
                    rowpass[...],
                    colw[...],
                    (((1,), (1,)), ((), ())),
                    preferred_element_type=F32,
                )
            )
        pixels = pix_b[b].astype(F32)
        value = pixels * (1.0 + fields[0] * inverse_cover) + fields[1] * inverse_cover
        tile_b[b] = value.astype(BF16)
        return carry

    lax.fori_loop(0, BD_, correct, 0)
    tiles = pltpu.make_async_copy(tile_b, tile_h, out_sem.at[1])
    tiles.start()

    for sweep in range(SWEEPS):
        for side in range(2):
            for piece in range(2):
                halo_copy(sweep, side, piece).wait_send()
        for part in range(2):
            for k in range(1, NB):
                part_copy(sweep, part, k).wait_send()

    def sent_pay(k, carry):
        pay_copy(k).wait_send()
        return carry

    lax.fori_loop(1, NG, sent_pay, 0)
    save.wait()
    tiles.wait()


def per_device(
    prior_grids,
    pif_rhs,
    pif_diagonal,
    pif_cross,
    pif_coupling,
    neighbour_offset,
    neighbour_count,
    tile_route,
    tile_window,
    tile_pixels,
):
    def pairs(x):
        return x.reshape(GD, BD_, 2, 32, 128).transpose(0, 1, 3, 2, 4).reshape(GD, BD_, 64, 128)

    prior = pairs(prior_grids)
    rhs = pairs(pif_rhs)
    diag = pairs(pif_diagonal)
    cross = (
        pif_cross.reshape(2, 8, BD_, 32, 128).transpose(2, 0, 3, 1, 4).reshape(BD_, 2, 256, 128)
    )
    coupling = (
        pif_coupling.reshape(GD, SLOTS, BD_, 32, 128)
        .transpose(0, 2, 3, 1, 4)
        .reshape(GD, BD_, 256, 128)
    )
    any_ = pl.BlockSpec(memory_space=pl.ANY)
    vmem = pl.BlockSpec(memory_space=pltpu.VMEM)
    smem = pl.BlockSpec(memory_space=pltpu.SMEM)
    dma = pltpu.SemaphoreType.DMA
    balanced, tiles = pl.pallas_call(
        kernel,
        out_shape=(
            jax.ShapeDtypeStruct((GD, BD_, 64, 128), F32),
            jax.ShapeDtypeStruct((BD_, PIX, PIX), BF16),
        ),
        in_specs=[smem, smem, any_, any_, any_, any_, any_, vmem, vmem, any_],
        out_specs=(any_, any_),
        scratch_shapes=[
            pltpu.VMEM((GD, BD_, 64, 128), F32),
            pltpu.VMEM((GD, BD_, 64, 128), F32),
            pltpu.VMEM((GD, BD_, 64, 128), F32),
            pltpu.VMEM((BD_, 2, 256, 128), F32),
            pltpu.VMEM((GD, BD_, 256, 128), BF16),
            pltpu.VMEM((BD_, PIX, PIX), BF16),
            pltpu.VMEM((GD, BD_, 64, 128), F32),
            pltpu.VMEM((BD_, PIX, PIX), BF16),
            pltpu.VMEM((2, GD + 2 * REACH, BD_, 2, 4, 8, 128), F32),
            pltpu.VMEM((GD + 2 * REACH, BD_, 4, 8, 128), F32),
            pltpu.VMEM((GD, BD_, SLOTS, 4, 8, 128), F32),
            pltpu.VMEM((GD, BD_, 4, 8, 128), F32),
            pltpu.VMEM((512, 128), F32),
            pltpu.VMEM((512, 128), F32),
            pltpu.VMEM((2, 32, 128), F32),
            pltpu.VMEM((SWEEPS, 2, 2, REACH, BD_, 32, 128), BF16),
            pltpu.VMEM((SWEEPS, 2, 2, REACH, BD_, 32, 128), BF16),
            pltpu.VMEM((SWEEPS, 2, 32, 128), F32),
            pltpu.VMEM((SWEEPS, 2, NB - 1, 32, 128), F32),
            pltpu.VMEM((NG, 128), I32),
            pltpu.SMEM((NG, 128), I32),
            pltpu.VMEM((NG, 32, 128), BF16),
            pltpu.VMEM((NG, 32, 128), BF16),
            pltpu.VMEM((PIX, 1024), BF16),
            pltpu.VMEM((PIX, 1024), BF16),
            pltpu.VMEM((24, 256, 256), BF16),
            pltpu.VMEM((PIX, 1024), BF16),
            dma((6,)),
            dma((2,)),
            dma((SWEEPS, 2, 2)),
            dma((SWEEPS, 2, 2)),
            dma((SWEEPS, 2, NB - 1)),
            dma((SWEEPS, 2, NB - 1)),
            dma((NG,)),
            dma((NG,)),
            dma,
            dma,
        ],
        compiler_params=pltpu.CompilerParams(
            collective_id=0, has_side_effects=True, vmem_limit_bytes=60 * 1024 * 1024
        ),
        name="balance",
    )(
        neighbour_offset.T,
        neighbour_count,
        prior,
        rhs,
        diag,
        cross,
        coupling,
        tile_route.T,
        tile_window.transpose(1, 2, 0),
        tile_pixels[0],
    )
    balanced = (
        balanced.reshape(GD, BD_, 32, 2, 128)
        .transpose(0, 1, 3, 2, 4)
        .reshape(GD, BD_, 2, 4096)
    )
    return (balanced, tiles[None])


def solution(mesh):
    placed = (
        P("gran", "band", None, None),
        P("gran", "band", None, None),
        P("gran", "band", None, None),
        P("gran", "band", None),
        P("gran", None, "band", None),
        P("gran", None),
        P("gran"),
        P(),
        P(),
        P("gran", "band", None, None),
    )
    return jax.shard_map(
        per_device,
        mesh=mesh,
        in_specs=placed,
        out_specs=(P("gran", "band", None, None), P("gran", "band", None, None)),
        check_vma=False,
    )
```

```python
import jax
import jax.numpy as jnp
from jax import lax
from jax.experimental import pallas as pl
from jax.experimental.pallas import tpu as pltpu
from jax.sharding import PartitionSpec as P

MESH = pl.DeviceIdType.MESH
F32 = jnp.float32
BF16 = jnp.bfloat16
I32 = jnp.int32

BANDS = 12
PATCH = 8
REACH = 4
SWEEPS = 3
SP = 32
ROBUST = 0.3 * BANDS * PATCH * PATCH

GD = 16
BD_ = 3
NG = 32
NB = 4
SLOTS = 8
PIX = 256
WIN = 16
FIRST_MAX = 64 - WIN
FAR = 1000.0
FAR_STEPS = 4


def iota(shape, dim):
    return lax.broadcasted_iota(I32, shape, dim)


def dot(a, b):
    return jnp.dot(a, b, preferred_element_type=F32)


def butterfly(x, lane, width, op):
    size = x.shape[1]
    step = 1
    while step < width:
        other = jnp.where(
            (lane // step) % 2 == 0,
            pltpu.roll(x, size - step, axis=1),
            pltpu.roll(x, step, axis=1),
        )
        x = op(x, other)
        step *= 2
    return x


def far_tap(d):
    return ((-0.5 * d + 2.5) * d - 4.0) * d + 2.0


def near_tap(d):
    return (1.5 * d - 2.5) * d * d + 1.0


PARTS = ((4, 8), (0, 4), (12, 4))


def packing(part):
    count = PARTS[part][1]
    blocks = 16 // count
    return count, blocks, 64 // blocks


def kernel(
    off_h,
    cnt_h,
    prior_h,
    rhs_h,
    diag_h,
    cross_h,
    coup_h,
    route_h,
    win_h,
    pix_h,
    bal_h,
    tile_h,
    off_s,
    cnt_s,
    route_v,
    win_v,
    prior_b,
    rhs_b,
    diag_b,
    cross_b,
    coup_b,
    pix_b,
    out_b,
    tile_b,
    grids,
    resp,
    coup,
    cterm,
    disp,
    spread,
    weight,
    halo_out,
    halo_in,
    part_out,
    part_in,
    tab_v,
    tab_s,
    pay_out,
    pay_in,
    roww,
    colw,
    diagonal,
    rowpass,
    in_sem,
    out_sem,
    hs_sem,
    hr_sem,
    ps_sem,
    pr_sem,
    as_sem,
    ar_sem,
    tab_sem,
    own_sem,
    far_sem,
):
    me = lax.axis_index("gran")
    mb = lax.axis_index("band")
    right = lax.rem(me + 1, NG)
    left = lax.rem(me + NG - 1, NG)

    barrier = pltpu.get_barrier_semaphore()
    for other in (left, right):
        pl.semaphore_signal(barrier, inc=1, device_id=(other, mb), device_id_type=MESH)
    for k in range(1, NB):
        pl.semaphore_signal(
            barrier, inc=1, device_id=(me, lax.rem(mb + k, NB)), device_id_type=MESH
        )

    def far_signal(step):
        distance = 1 << step
        for side, shift in enumerate((distance, NG - distance)):
            pl.semaphore_signal(
                far_sem.at[step, side],
                inc=1,
                device_id=(lax.rem(me + shift, NG), mb),
                device_id_type=MESH,
            )

    def far_wait(step):
        for side in range(2):
            pl.semaphore_wait(far_sem.at[step, side], 1)

    ends = (pl.ds(0, REACH), pl.ds(GD - REACH, REACH))
    middle = pl.ds(REACH, GD - 2 * REACH)
    pairs = [(prior_h.at[part], prior_b.at[part]) for part in (*ends, middle)]
    pairs += [
        (off_h, off_s),
        (cnt_h, cnt_s),
        (coup_h, coup_b),
        (diag_h, diag_b),
        (cross_h, cross_b),
        (rhs_h, rhs_b),
        (route_h, route_v),
        (win_h, win_v),
        (pix_h, pix_b),
    ]
    loads = [
        pltpu.make_async_copy(src, dst, in_sem.at[n]) for n, (src, dst) in enumerate(pairs)
    ]
    for load in loads[:2]:
        load.start()

    lane128 = iota((128, 128), 1)
    sub128 = iota((128, 128), 0)
    gather_table = ((sub128 % 64) // 8 == lane128 % 8).astype(F32).astype(BF16)
    spread_table = ((lane128 % 64) // 8 == sub128 % 8).astype(F32).astype(BF16)

    def take_prior(i):
        for b in range(BD_):
            for v in range(4):
                g0 = prior_b[i, b, pl.ds(2 * v, 8, stride=8), :]
                g1 = prior_b[i, b, pl.ds(2 * v + 1, 8, stride=8), :]
                grids[0, REACH + i, b, 0, v] = g0
                grids[0, REACH + i, b, 1, v] = g1
                resp[REACH + i, b, v] = g0 + g1

    def halo_rows(sweep, side, e, i):
        for b in range(BD_):
            halo_out[sweep, side, 0, e, b] = resp[REACH + i, b].reshape(32, 128).astype(BF16)
            halo_out[sweep, side, 1, e, b] = (
                grids[sweep % 2, REACH + i, b, 0].reshape(32, 128).astype(BF16)
            )

    for load in loads[:2]:
        load.wait()
    for load in loads[2:]:
        load.start()
    for side, base in ((1, 0), (0, GD - REACH)):

        def first_halo(e, carry, side=side, base=base):
            take_prior(base + e)
            halo_rows(0, side, e, base + e)
            return carry

        lax.fori_loop(0, REACH, first_halo, 0)

    pl.semaphore_wait(barrier, 2 + NB - 1)

    def halo_copy(sweep, side, piece):
        return pltpu.make_async_remote_copy(
            src_ref=halo_out.at[sweep, side, piece],
            dst_ref=halo_in.at[sweep, side, piece],
            send_sem=hs_sem.at[sweep, side, piece],
            recv_sem=hr_sem.at[sweep, side, piece],
            device_id=(right if side == 0 else left, mb),
            device_id_type=MESH,
        )

    def start_halo(sweep, side):
        for piece in range(2):
            halo_copy(sweep, side, piece).start()

    def part_copy(sweep, part, k):
        return pltpu.make_async_remote_copy(
            src_ref=part_out.at[sweep, part, pl.ds(0, packing(part)[2])],
            dst_ref=part_in.at[sweep, part, k - 1, pl.ds(0, packing(part)[2])],
            send_sem=ps_sem.at[sweep, part, k - 1],
            recv_sem=pr_sem.at[sweep, part, k - 1],
            device_id=(me, lax.rem(mb + k, NB)),
            device_id_type=MESH,
        )

    start_halo(0, 0)
    start_halo(0, 1)
    far_signal(0)

    for load in loads[2:5]:
        load.wait()

    def rest(k, carry):
        take_prior(REACH + k)
        return carry

    lax.fori_loop(0, GD - 2 * REACH, rest, 0)

    for part in range(3):
        count, blocks, rows = packing(part)
        lane_block = iota((rows, 128), 1) // 8
        slot = (lane_block // count) * (SLOTS // blocks) + iota((rows, 128), 0) // 8
        counts = jnp.zeros((rows, 128), I32)
        for k in range(count):
            counts = jnp.where(lane_block % count == k, cnt_s[PARTS[part][0] + k], counts)
        weight[part, :rows] = (slot < counts).astype(F32)

    def disparity(part, sweep):
        base = PARTS[part][0]
        count, blocks, height = packing(part)

        def one(k, carry):
            i = base + k
            own = [resp[REACH + i, b] for b in range(BD_)]
            for s in range(SLOTS):
                n = REACH + i + off_s[s, i]
                total = None
                for b in range(BD_):
                    diff = own[b] - resp[n, b]
                    square = diff * diff
                    total = square if total is None else total + square
                disp[pl.ds(pl.multiple_of(k * 64 + s * 8, 8), 8), :] = (
                    total[0] + total[1] + total[2] + total[3]
                )
            return carry

        lax.fori_loop(0, count, one, 0)
        sums = dot(disp[: count * 64].astype(BF16), gather_table)
        packed = jnp.zeros((height, 128), F32)
        lane_block = iota((height, 128), 1) // 8
        for k in range(count):
            for h in range(blocks):
                at = k * 64 + h * height
                packed = jnp.where(lane_block == h * count + k, sums[at : at + height], packed)
        part_out[sweep, part, :height] = packed.astype(BF16)
        for k in (2, 1, 3):
            part_copy(sweep, part, k).start()

    def solve(part, sweep):
        base = PARTS[part][0]
        count, blocks, height = packing(part)
        now, later = sweep % 2, (sweep + 1) % 2
        last = sweep == SWEEPS - 1
        for k in range(1, NB):
            part_copy(sweep, part, k).wait_recv()
        total = part_out[sweep, part, :height].astype(F32)
        for k in range(NB - 1):
            total = total + part_in[sweep, part, k, :height].astype(F32)
        robust = weight[part, :height] / (1.0 + total * (1.0 / ROBUST))
        lane_block = iota((height, 128), 1) // 8
        rows = []
        for k in range(count):
            for h in range(blocks):
                rows.append(jnp.where(lane_block == h * count + k, robust, 0.0))
        spread[: count * 64] = dot(jnp.concatenate(rows, axis=0).astype(BF16), spread_table)

        def one(k, carry):
            i = base + k
            places = [REACH + i + off_s[s, i] for s in range(SLOTS)]
            for b in range(BD_):
                sigma = drive0 = drive1 = None
                for s in range(SLOTS):
                    rob = spread[pl.ds(pl.multiple_of(k * 64 + s * 8, 8), 8), :]
                    eff = rob[None] * coup[i, b, s]
                    add0 = eff * grids[now, places[s], b, 0]
                    add1 = eff * grids[now, places[s], b, 1]
                    if s == 0:
                        sigma, drive0, drive1 = eff, add0, add1
                    else:
                        sigma, drive0, drive1 = sigma + eff, drive0 + add0, drive1 + add1
                for v in range(4):
                    even = pl.ds(2 * v, 8, stride=8)
                    odd = pl.ds(2 * v + 1, 8, stride=8)
                    r0 = rhs_b[i, b, even, :] + drive0[v]
                    r1 = rhs_b[i, b, odd, :] + drive1[v]
                    first = diag_b[i, b, even, :] + sigma[v]
                    second = diag_b[i, b, odd, :] + sigma[v]
                    cross = cterm[i, b, v]
                    inverse = 1.0 / (first * second - cross * cross)
                    g0 = (second * r0 - cross * r1) * inverse
                    g1 = (first * r1 - cross * r0) * inverse
                    if last:
                        out_b[i, b, even, :] = g0
                        out_b[i, b, odd, :] = g1
                    else:
                        grids[later, REACH + i, b, 0, v] = g0
                        grids[later, REACH + i, b, 1, v] = g1
                        resp[REACH + i, b, v] = g0 + g1
            if part > 0 and not last:
                halo_rows(sweep + 1, 2 - part, k, i)
            return carry

        lax.fori_loop(0, count, one, 0)
        if part > 0 and not last:
            start_halo(sweep + 1, 2 - part)

    def take_responses(sweep, side):
        halo_copy(sweep, side, 0).wait_recv()

        def one(e, carry):
            for b in range(BD_):
                value = halo_in[sweep, side, 0, e, b].astype(F32)
                resp[e + side * (REACH + GD), b] = value.reshape(4, 8, 128)
            return carry

        lax.fori_loop(0, REACH, one, 0)

    def take_grids(sweep, side):
        now = sweep % 2
        halo_copy(sweep, side, 1).wait_recv()

        def one(e, carry):
            place = e + side * (REACH + GD)
            for b in range(BD_):
                g0 = halo_in[sweep, side, 1, e, b].astype(F32).reshape(4, 8, 128)
                grids[now, place, b, 0] = g0
                grids[now, place, b, 1] = resp[place, b] - g0
            return carry

        lax.fori_loop(0, REACH, one, 0)

    def take_coupling():
        row = iota((256, 256), 0)
        source = (4 * (row % 8) + (row // 8) % 4) * 8 + row // 32
        order = (iota((256, 256), 1) == source).astype(F32).astype(BF16)

        def one(i, carry):
            for b in range(BD_):
                both = jnp.concatenate([coup_b[i, b], coup_b[i + 8, b]], axis=1)
                moved = dot(order, both)
                coup[i, b] = moved[:, :128].reshape(SLOTS, 4, 8, 128)
                coup[i + 8, b] = moved[:, 128:].reshape(SLOTS, 4, 8, 128)
            return carry

        lax.fori_loop(0, GD // 2, one, 0)

    def take_cross():
        def one(half, carry):
            for g in range(8):
                i = half * 8 + g
                for b in range(BD_):
                    for v in range(4):
                        d0 = diag_b[i, b, pl.ds(2 * v, 8, stride=8), :]
                        d1 = diag_b[i, b, pl.ds(2 * v + 1, 8, stride=8), :]
                        value = cross_b[b, half, pl.ds(8 * v + g, 8, stride=32), :]
                        cterm[i, b, v] = value * jnp.sqrt(d0 * d1)
            return carry

        lax.fori_loop(0, 2, one, 0)

    def send_table():
        block = pl.multiple_of((me // 8) * 128, 128)
        turn = lax.rem(128 - lax.rem(me, 8) * 16, 128)
        lane = iota((32, 128), 1)
        tile = iota((32, 128), 0)

        def own(ref_rows):
            pair = []
            for route in range(2):
                row = jnp.broadcast_to(ref_rows(route, pl.ds(block, 128)), (32, 128))
                row = pltpu.roll(row, turn, axis=1)
                pair.append(pltpu.roll(row, 16, axis=1) if route else row)
            return jnp.where(lane < 16, pair[0], pair[1])

        routes = own(lambda route, cols: route_v[pl.ds(route, 1), cols])
        starts = [
            own(lambda route, cols, c=c: win_v[route, pl.ds(c, 1), cols]) for c in range(2)
        ]
        match = (routes == tile) & (lane < 32)
        low = butterfly(jnp.where(match, lane, 99), lane, 32, jnp.minimum)
        high = butterfly(jnp.where(match, lane, -1), lane, 32, jnp.maximum)
        table = jnp.zeros((32, 128), I32)
        for rank, chosen in enumerate((low, high)):
            picks = [
                butterfly(
                    jnp.where((lane == chosen) & (lane < 32), start, 0), lane, 32, jnp.add
                )
                for start in starts
            ]
            valid = (chosen >= 0) & (chosen < 32)
            granule = jnp.where(valid, chosen % 16, 0)
            first = [jnp.clip(pick // SP - 1, 0, FIRST_MAX) for pick in picks]
            for column, value in enumerate((granule, first[0] // 2, first[1])):
                table = jnp.where(lane == rank * 3 + column, value, table)
        tab_v[...] = table
        copy = pltpu.make_async_copy(tab_v, tab_s, tab_sem)
        copy.start()
        copy.wait()

    def weights(coord, ref):
        lane = iota((8, 512), 1)
        place = lane % 16
        match = []
        for route in range(2):
            row = jnp.broadcast_to(route_v[pl.ds(route, 1), :], (8, 512))
            match.append(row == me)
        low = jnp.minimum(
            jnp.where(match[0], place, 99), jnp.where(match[1], place + 16, 99)
        )
        high = jnp.maximum(
            jnp.where(match[0], place, -1), jnp.where(match[1], place + 16, -1)
        )
        low = butterfly(low, lane, 16, jnp.minimum)
        high = butterfly(high, lane, 16, jnp.maximum)
        total = jnp.sum(
            (match[0].astype(F32) + match[1].astype(F32))[0:1], axis=1, keepdims=True
        )
        for rank, chosen in enumerate((low, high)):
            live = (chosen < 32) if rank == 0 else (high != low) & (chosen >= 0)
            if True:
                pick = jnp.zeros((8, 512), I32)
                for route in range(2):
                    row = jnp.broadcast_to(win_v[route, pl.ds(coord, 1), :], (8, 512))
                    pick = pick + jnp.where(chosen == place + 16 * route, row, 0)
                pick = butterfly(pick, lane, 16, jnp.add)
                first = jnp.clip(pick // SP - 1, 0, FIRST_MAX)
                if coord == 0:
                    knot = (first // 2) * 2 + 2 * (place % 8) + place // 8
                else:
                    knot = first + place
                knot_f = knot.astype(F32)
                extra = jnp.where(
                    knot == 0, -1.0, jnp.where(knot == 63, 64.0, FAR)
                )
                start = pick.astype(F32) * (1.0 / SP)
                lead = start - knot_f
                lead_extra = start - extra

                def rows(block, carry, ref=ref, rank=rank, lead=lead, lead_extra=lead_extra,
                         live=live, coord=coord):
                    parts = []
                    for h in range(2):
                        pixel = (
                            iota((8, 512), 0) + (block * 16 + h * 8)
                        ).astype(F32) * (1.0 / SP)
                        d = jnp.abs(lead + pixel)
                        w = jnp.where(d <= 1.0, near_tap(d), far_tap(d))
                        w = jnp.where(d < 2.0, w, 0.0)
                        d2 = jnp.abs(lead_extra + pixel)
                        w = w + jnp.where(d2 < 2.0, far_tap(d2), 0.0)
                        if coord == 1:
                            w = jnp.where(live, w, 0.0)
                        parts.append(w)
                    ref[pl.ds(pl.multiple_of(block * 16, 16), 16), rank * 512 : rank * 512 + 512] = (
                        jnp.concatenate(parts, axis=0).astype(BF16)
                    )
                    return carry

                lax.fori_loop(0, PIX // 16, rows, 0)
        return 1.0 / total

    def clear_diagonal():
        def one(n, carry):
            diagonal[n] = jnp.zeros((256, 256), BF16)
            return carry

        lax.fori_loop(0, 24, one, 0)

    cover = None
    for sweep in range(SWEEPS):
        order = (1, 2) if sweep % 2 == 0 else (2, 1)
        disparity(0, sweep)
        if sweep == 0:
            loads[5].wait()
            take_coupling()
        elif sweep == 1:
            far_wait(1)
            far_signal(2)
            loads[9].wait()
            loads[10].wait()
            weights(0, roww)
        else:
            cover = weights(1, colw)
        for step, part in enumerate(order):
            take_responses(sweep, part - 1)
            if step == 0 and sweep < 2:
                far_wait(2 * sweep)
                far_signal(2 * sweep + 1)
            disparity(part, sweep)
        if sweep == 0:
            loads[6].wait()
            loads[7].wait()
            take_cross()
            loads[8].wait()
        solve(0, sweep)
        if sweep == 1:
            send_table()
        elif sweep == 2:
            clear_diagonal()
            far_wait(3)
        for part in order:
            take_grids(sweep, part - 1)
            solve(part, sweep)
    inverse_cover = cover

    save = pltpu.make_async_copy(out_b, bal_h, out_sem.at[0])
    save.start()

    lane8 = iota((8, 128), 1)
    lane_band = (lane8 % 64) // 16

    def fill(t, carry):
        for rank in range(2):
            granule = tab_s[t, rank * 3]
            row = tab_s[t, rank * 3 + 1]
            column = tab_s[t, rank * 3 + 2]
            halves = []
            for c in range(2):
                value = None
                for b in range(BD_):
                    x = out_b[granule, b, pl.ds(2 * row + c, 8, stride=2), :]
                    x = pltpu.roll(x, lax.rem(b * 16 + 128 - column, 128), axis=1)
                    value = x if value is None else jnp.where(lane_band == b, x, value)
                halves.append(value)
            pay_out[t, rank * 16 : rank * 16 + 16, :] = jnp.concatenate(halves, axis=0).astype(BF16)
        return carry

    lax.fori_loop(0, NG, fill, 0)

    def pay_copy(k):
        return pltpu.make_async_remote_copy(
            src_ref=pay_out.at[lax.rem(me + k, NG)],
            dst_ref=pay_in.at[me],
            send_sem=as_sem.at[k],
            recv_sem=ar_sem.at[k],
            device_id=(lax.rem(me + k, NG), mb),
            device_id_type=MESH,
        )

    def send_pay(k, carry):
        pay_copy(k).start()
        return carry

    lax.fori_loop(1, NG, send_pay, 0)
    own_copy = pltpu.make_async_copy(pay_out.at[me], pay_in.at[me], own_sem)
    own_copy.start()
    loads[11].wait()
    own_copy.wait()

    def take_pay(k, carry):
        pltpu.make_async_remote_copy(
            src_ref=pay_out.at[lax.rem(me + k, NG)],
            dst_ref=pay_in.at[lax.rem(me + NG - k, NG)],
            send_sem=as_sem.at[k],
            recv_sem=ar_sem.at[k],
            device_id=(lax.rem(me + k, NG), mb),
            device_id_type=MESH,
        ).wait_recv()
        return carry

    lax.fori_loop(1, NG, take_pay, 0)

    def expand(group, carry):
        rank = group // 2
        base = lax.rem(group, 2) * 16
        for s in range(16):
            block = pay_in[base + s, pl.ds(pl.multiple_of(rank * 16, 16), 16), :].astype(F32)
            for c in range(2):
                x = block[c * 8 : c * 8 + 8]
                for b in range(BD_):
                    parts = []
                    for parity in range(2):
                        turn = ((s % 8) * 16 - parity * 64 - b * 16) % 128
                        y = pltpu.roll(x, turn, axis=1) if turn else x
                        parts.append(jnp.where(lane8 // 16 == s % 8, y, 0.0))
                    diagonal[
                        group * 6 + b * 2 + c,
                        s * 16 : s * 16 + 16,
                        (s // 8) * 128 : (s // 8) * 128 + 128,
                    ] = jnp.concatenate(parts, axis=0).astype(BF16)
        return carry

    lax.fori_loop(0, 4, expand, 0)

    def correct(b, carry):
        fields = []
        for c in range(2):
            for group in range(4):
                cols = slice(group * 256, group * 256 + 256)
                rowpass[:, cols] = dot(roww[:, cols], diagonal[group * 6 + b * 2 + c]).astype(BF16)
            fields.append(
                lax.dot_general(
                    rowpass[...],
                    colw[...],
                    (((1,), (1,)), ((), ())),
                    preferred_element_type=F32,
                )
            )
        pixels = pix_b[b].astype(F32)
        value = pixels * (1.0 + fields[0] * inverse_cover) + fields[1] * inverse_cover
        tile_b[b] = value.astype(BF16)
        return carry

    lax.fori_loop(0, BD_, correct, 0)
    tiles = pltpu.make_async_copy(tile_b, tile_h, out_sem.at[1])
    tiles.start()

    for sweep in range(SWEEPS):
        for side in range(2):
            for piece in range(2):
                halo_copy(sweep, side, piece).wait_send()
        for part in range(3):
            for k in range(1, NB):
                part_copy(sweep, part, k).wait_send()

    def sent_pay(k, carry):
        pay_copy(k).wait_send()
        return carry

    lax.fori_loop(1, NG, sent_pay, 0)
    save.wait()
    tiles.wait()


def per_device(
    prior_grids,
    pif_rhs,
    pif_diagonal,
    pif_cross,
    pif_coupling,
    neighbour_offset,
    neighbour_count,
    tile_route,
    tile_window,
    tile_pixels,
):
    def pairs(x):
        return x.reshape(GD, BD_, 2, 32, 128).transpose(0, 1, 3, 2, 4).reshape(GD, BD_, 64, 128)

    prior = pairs(prior_grids)
    rhs = pairs(pif_rhs)
    diag = pairs(pif_diagonal)
    cross = (
        pif_cross.reshape(2, 8, BD_, 32, 128).transpose(2, 0, 3, 1, 4).reshape(BD_, 2, 256, 128)
    )
    coupling = (
        pif_coupling.reshape(GD, SLOTS, BD_, 32, 128)
        .transpose(0, 2, 3, 1, 4)
        .reshape(GD, BD_, 256, 128)
    )
    any_ = pl.BlockSpec(memory_space=pl.ANY)
    dma = pltpu.SemaphoreType.DMA
    balanced, tiles = pl.pallas_call(
        kernel,
        out_shape=(
            jax.ShapeDtypeStruct((GD, BD_, 64, 128), F32),
            jax.ShapeDtypeStruct((BD_, PIX, PIX), BF16),
        ),
        in_specs=[any_] * 10,
        out_specs=(any_, any_),
        scratch_shapes=[
            pltpu.SMEM((SLOTS, GD), I32),
            pltpu.SMEM((GD,), I32),
            pltpu.VMEM((2, NG * GD), I32),
            pltpu.VMEM((2, 2, NG * GD), I32),
            pltpu.VMEM((GD, BD_, 64, 128), F32),
            pltpu.VMEM((GD, BD_, 64, 128), F32),
            pltpu.VMEM((GD, BD_, 64, 128), F32),
            pltpu.VMEM((BD_, 2, 256, 128), F32),
            pltpu.VMEM((GD, BD_, 256, 128), BF16),
            pltpu.VMEM((BD_, PIX, PIX), BF16),
            pltpu.VMEM((GD, BD_, 64, 128), F32),
            pltpu.VMEM((BD_, PIX, PIX), BF16),
            pltpu.VMEM((2, GD + 2 * REACH, BD_, 2, 4, 8, 128), F32),
            pltpu.VMEM((GD + 2 * REACH, BD_, 4, 8, 128), F32),
            pltpu.VMEM((GD, BD_, SLOTS, 4, 8, 128), F32),
            pltpu.VMEM((GD, BD_, 4, 8, 128), F32),
            pltpu.VMEM((512, 128), F32),
            pltpu.VMEM((512, 128), F32),
            pltpu.VMEM((3, 32, 128), F32),
            pltpu.VMEM((SWEEPS, 2, 2, REACH, BD_, 32, 128), BF16),
            pltpu.VMEM((SWEEPS, 2, 2, REACH, BD_, 32, 128), BF16),
            pltpu.VMEM((SWEEPS, 3, 32, 128), BF16),
            pltpu.VMEM((SWEEPS, 3, NB - 1, 32, 128), BF16),
            pltpu.VMEM((NG, 128), I32),
            pltpu.SMEM((NG, 128), I32),
            pltpu.VMEM((NG, 32, 128), BF16),
            pltpu.VMEM((NG, 32, 128), BF16),
            pltpu.VMEM((PIX, 1024), BF16),
            pltpu.VMEM((PIX, 1024), BF16),
            pltpu.VMEM((24, 256, 256), BF16),
            pltpu.VMEM((PIX, 1024), BF16),
            dma((12,)),
            dma((2,)),
            dma((SWEEPS, 2, 2)),
            dma((SWEEPS, 2, 2)),
            dma((SWEEPS, 3, NB - 1)),
            dma((SWEEPS, 3, NB - 1)),
            dma((NG,)),
            dma((NG,)),
            dma,
            dma,
            pltpu.SemaphoreType.REGULAR((FAR_STEPS, 2)),
        ],
        compiler_params=pltpu.CompilerParams(
            collective_id=0, has_side_effects=True, vmem_limit_bytes=60 * 1024 * 1024
        ),
        name="balance",
    )(
        neighbour_offset.T,
        neighbour_count,
        prior,
        rhs,
        diag,
        cross,
        coupling,
        tile_route.T,
        tile_window.transpose(1, 2, 0),
        tile_pixels[0],
    )
    balanced = (
        balanced.reshape(GD, BD_, 32, 2, 128)
        .transpose(0, 1, 3, 2, 4)
        .reshape(GD, BD_, 2, 4096)
    )
    return (balanced, tiles[None])


def solution(mesh):
    placed = (
        P("gran", "band", None, None),
        P("gran", "band", None, None),
        P("gran", "band", None, None),
        P("gran", "band", None),
        P("gran", None, "band", None),
        P("gran", None),
        P("gran"),
        P(),
        P(),
        P("gran", "band", None, None),
    )
    return jax.shard_map(
        per_device,
        mesh=mesh,
        in_specs=placed,
        out_specs=(P("gran", "band", None, None), P("gran", "band", None, None)),
        check_vma=False,
    )
```

```python
import jax
import jax.numpy as jnp
from jax import lax
from jax.experimental import pallas as pl
from jax.experimental.pallas import tpu as pltpu
from jax.sharding import PartitionSpec as P

MESH = pl.DeviceIdType.MESH
F32 = jnp.float32
BF16 = jnp.bfloat16
I32 = jnp.int32

BANDS = 12
PATCH = 8
REACH = 4
SWEEPS = 3
SP = 32
ROBUST = 0.3 * BANDS * PATCH * PATCH

GD = 16
BD_ = 3
NG = 32
NB = 4
SLOTS = 8
PIX = 256
WIN = 16
FIRST_MAX = 64 - WIN
FAR = 1000.0
FAR_STEPS = 4
TILE_VMEM = 60 * 1024 * 1024


def iota(shape, dim):
    return lax.broadcasted_iota(I32, shape, dim)


def dot(a, b):
    return jnp.dot(a, b, preferred_element_type=F32)


def butterfly(x, lane, width, op):
    size = x.shape[1]
    step = 1
    while step < width:
        other = jnp.where(
            (lane // step) % 2 == 0,
            pltpu.roll(x, size - step, axis=1),
            pltpu.roll(x, step, axis=1),
        )
        x = op(x, other)
        step *= 2
    return x


def far_tap(d):
    return ((-0.5 * d + 2.5) * d - 4.0) * d + 2.0


def near_tap(d):
    return (1.5 * d - 2.5) * d * d + 1.0


PARTS = ((4, 8), (0, 4), (12, 4))


def packing(part):
    count = PARTS[part][1]
    blocks = 16 // count
    return count, blocks, 64 // blocks


def kernel(
    off_h,
    cnt_h,
    prior_h,
    rhs_h,
    diag_h,
    cross_h,
    coup_h,
    route_h,
    win_h,
    bal_h,
    pay_in,
    roww_h,
    colw_h,
    cover_h,
    off_s,
    cnt_s,
    route_v,
    win_v,
    prior_b,
    rhs_b,
    diag_b,
    cross_b,
    coup_b,
    out_b,
    grids,
    resp,
    coup,
    cterm,
    disp,
    spread,
    weight,
    halo_out,
    halo_in,
    part_out,
    part_in,
    tab_v,
    tab_s,
    pay_out,
    roww,
    colw,
    colt,
    cover_v,
    in_sem,
    out_sem,
    hs_sem,
    hr_sem,
    ps_sem,
    pr_sem,
    as_sem,
    ar_sem,
    tab_sem,
    own_sem,
    far_sem,
):
    me = lax.axis_index("gran")
    mb = lax.axis_index("band")
    right = lax.rem(me + 1, NG)
    left = lax.rem(me + NG - 1, NG)

    barrier = pltpu.get_barrier_semaphore()
    for other in (left, right):
        pl.semaphore_signal(barrier, inc=1, device_id=(other, mb), device_id_type=MESH)
    for k in range(1, NB):
        pl.semaphore_signal(
            barrier, inc=1, device_id=(me, lax.rem(mb + k, NB)), device_id_type=MESH
        )

    def far_signal(step):
        distance = 1 << step
        for side, shift in enumerate((distance, NG - distance)):
            pl.semaphore_signal(
                far_sem.at[step, side],
                inc=1,
                device_id=(lax.rem(me + shift, NG), mb),
                device_id_type=MESH,
            )

    def far_wait(step):
        for side in range(2):
            pl.semaphore_wait(far_sem.at[step, side], 1)

    ends = (pl.ds(0, REACH), pl.ds(GD - REACH, REACH))
    middle = pl.ds(REACH, GD - 2 * REACH)
    pairs = [(prior_h.at[part], prior_b.at[part]) for part in (*ends, middle)]
    pairs += [
        (off_h, off_s),
        (cnt_h, cnt_s),
        (coup_h, coup_b),
        (diag_h, diag_b),
        (cross_h, cross_b),
        (rhs_h, rhs_b),
        (route_h, route_v),
        (win_h, win_v),
    ]
    loads = [
        pltpu.make_async_copy(src, dst, in_sem.at[n]) for n, (src, dst) in enumerate(pairs)
    ]
    for load in loads[:2]:
        load.start()

    lane128 = iota((128, 128), 1)
    sub128 = iota((128, 128), 0)
    gather_table = ((sub128 % 64) // 8 == lane128 % 8).astype(F32).astype(BF16)
    spread_table = ((lane128 % 64) // 8 == sub128 % 8).astype(F32).astype(BF16)

    def take_prior(i):
        for b in range(BD_):
            for v in range(4):
                g0 = prior_b[i, b, pl.ds(2 * v, 8, stride=8), :]
                g1 = prior_b[i, b, pl.ds(2 * v + 1, 8, stride=8), :]
                grids[0, REACH + i, b, 0, v] = g0
                grids[0, REACH + i, b, 1, v] = g1
                resp[REACH + i, b, v] = g0 + g1

    def halo_rows(sweep, side, e, i):
        for b in range(BD_):
            halo_out[sweep, side, 0, e, b] = resp[REACH + i, b].reshape(32, 128).astype(BF16)
            halo_out[sweep, side, 1, e, b] = (
                grids[sweep % 2, REACH + i, b, 0].reshape(32, 128).astype(BF16)
            )

    for load in loads[:2]:
        load.wait()
    for load in loads[2:]:
        load.start()
    for side, base in ((1, 0), (0, GD - REACH)):

        def first_halo(e, carry, side=side, base=base):
            take_prior(base + e)
            halo_rows(0, side, e, base + e)
            return carry

        lax.fori_loop(0, REACH, first_halo, 0)

    pl.semaphore_wait(barrier, 2 + NB - 1)

    def halo_copy(sweep, side, piece):
        whole = not isinstance(piece, jax.Array) and piece == REACH
        part = (sweep, side, 1) if whole else (sweep, side, 0, piece)
        return pltpu.make_async_remote_copy(
            src_ref=halo_out.at[part],
            dst_ref=halo_in.at[part],
            send_sem=hs_sem.at[sweep, side, piece],
            recv_sem=hr_sem.at[sweep, side, piece],
            device_id=(right if side == 0 else left, mb),
            device_id_type=MESH,
        )

    def part_copy(sweep, part, k):
        return pltpu.make_async_remote_copy(
            src_ref=part_out.at[sweep, part, pl.ds(0, packing(part)[2])],
            dst_ref=part_in.at[sweep, part, k - 1, pl.ds(0, packing(part)[2])],
            send_sem=ps_sem.at[sweep, part, k - 1],
            recv_sem=pr_sem.at[sweep, part, k - 1],
            device_id=(me, lax.rem(mb + k, NB)),
            device_id_type=MESH,
        )

    for piece in range(REACH + 1):
        for side in range(2):
            halo_copy(0, side, piece).start()
    far_signal(0)

    for load in loads[2:5]:
        load.wait()

    def rest(k, carry):
        take_prior(REACH + k)
        return carry

    lax.fori_loop(0, GD - 2 * REACH, rest, 0)

    for part in range(3):
        count, blocks, rows = packing(part)
        lane_block = iota((rows, 128), 1) // 8
        slot = (lane_block // count) * (SLOTS // blocks) + iota((rows, 128), 0) // 8
        counts = jnp.zeros((rows, 128), I32)
        for k in range(count):
            counts = jnp.where(lane_block % count == k, cnt_s[PARTS[part][0] + k], counts)
        weight[part, :rows] = (slot < counts).astype(F32)

    def disparity(part, sweep):
        base = PARTS[part][0]
        count, blocks, height = packing(part)

        def one(k, carry):
            i = base + k
            own = [resp[REACH + i, b] for b in range(BD_)]
            for s in range(SLOTS):
                n = REACH + i + off_s[s, i]
                total = None
                for b in range(BD_):
                    diff = own[b] - resp[n, b]
                    square = diff * diff
                    total = square if total is None else total + square
                disp[pl.ds(pl.multiple_of(k * 64 + s * 8, 8), 8), :] = (
                    total[0] + total[1] + total[2] + total[3]
                )
            return carry

        lax.fori_loop(0, count, one, 0)
        sums = dot(disp[: count * 64].astype(BF16), gather_table)
        packed = jnp.zeros((height, 128), F32)
        lane_block = iota((height, 128), 1) // 8
        for k in range(count):
            for h in range(blocks):
                at = k * 64 + h * height
                packed = jnp.where(lane_block == h * count + k, sums[at : at + height], packed)
        part_out[sweep, part, :height] = packed.astype(BF16)
        for k in (2, 1, 3):
            part_copy(sweep, part, k).start()

    def solve(part, sweep):
        base = PARTS[part][0]
        count, blocks, height = packing(part)
        now, later = sweep % 2, (sweep + 1) % 2
        last = sweep == SWEEPS - 1
        for k in range(1, NB):
            part_copy(sweep, part, k).wait_recv()
        total = part_out[sweep, part, :height].astype(F32)
        for k in range(NB - 1):
            total = total + part_in[sweep, part, k, :height].astype(F32)
        robust = weight[part, :height] / (1.0 + total * (1.0 / ROBUST))
        lane_block = iota((height, 128), 1) // 8
        rows = []
        for k in range(count):
            for h in range(blocks):
                rows.append(jnp.where(lane_block == h * count + k, robust, 0.0))
        spread[: count * 64] = dot(jnp.concatenate(rows, axis=0).astype(BF16), spread_table)

        def one(k, carry):
            i = base + k
            places = [REACH + i + off_s[s, i] for s in range(SLOTS)]
            for b in range(BD_):
                sigma = drive0 = drive1 = None
                for s in range(SLOTS):
                    rob = spread[pl.ds(pl.multiple_of(k * 64 + s * 8, 8), 8), :]
                    eff = rob[None] * coup[i, b, s]
                    add0 = eff * grids[now, places[s], b, 0]
                    add1 = eff * grids[now, places[s], b, 1]
                    if s == 0:
                        sigma, drive0, drive1 = eff, add0, add1
                    else:
                        sigma, drive0, drive1 = sigma + eff, drive0 + add0, drive1 + add1
                for v in range(4):
                    even = pl.ds(2 * v, 8, stride=8)
                    odd = pl.ds(2 * v + 1, 8, stride=8)
                    r0 = rhs_b[i, b, even, :] + drive0[v]
                    r1 = rhs_b[i, b, odd, :] + drive1[v]
                    first = diag_b[i, b, even, :] + sigma[v]
                    second = diag_b[i, b, odd, :] + sigma[v]
                    cross = cterm[i, b, v]
                    inverse = 1.0 / (first * second - cross * cross)
                    g0 = (second * r0 - cross * r1) * inverse
                    g1 = (first * r1 - cross * r0) * inverse
                    if last:
                        out_b[i, b, even, :] = g0
                        out_b[i, b, odd, :] = g1
                    else:
                        grids[later, REACH + i, b, 0, v] = g0
                        grids[later, REACH + i, b, 1, v] = g1
                        resp[REACH + i, b, v] = g0 + g1
            if part > 0 and not last:
                halo_rows(sweep + 1, 2 - part, k, i)
                halo_copy(sweep + 1, 2 - part, k).start()
            return carry

        lax.fori_loop(0, count, one, 0)
        if part > 0 and not last:
            halo_copy(sweep + 1, 2 - part, REACH).start()

    def take_responses(sweep, side):
        def one(e, carry):
            halo_copy(sweep, side, e).wait_recv()
            for b in range(BD_):
                value = halo_in[sweep, side, 0, e, b].astype(F32)
                resp[e + side * (REACH + GD), b] = value.reshape(4, 8, 128)
            return carry

        lax.fori_loop(0, REACH, one, 0)

    def take_grids(sweep, side):
        now = sweep % 2
        halo_copy(sweep, side, REACH).wait_recv()

        def one(e, carry):
            place = e + side * (REACH + GD)
            for b in range(BD_):
                g0 = halo_in[sweep, side, 1, e, b].astype(F32).reshape(4, 8, 128)
                grids[now, place, b, 0] = g0
                grids[now, place, b, 1] = resp[place, b] - g0
            return carry

        lax.fori_loop(0, REACH, one, 0)

    def take_coupling():
        row = iota((256, 256), 0)
        source = (4 * (row % 8) + (row // 8) % 4) * 8 + row // 32
        order = (iota((256, 256), 1) == source).astype(F32).astype(BF16)

        def one(i, carry):
            for b in range(BD_):
                both = jnp.concatenate([coup_b[i, b], coup_b[i + 8, b]], axis=1)
                moved = dot(order, both)
                coup[i, b] = moved[:, :128].reshape(SLOTS, 4, 8, 128)
                coup[i + 8, b] = moved[:, 128:].reshape(SLOTS, 4, 8, 128)
            return carry

        lax.fori_loop(0, GD // 2, one, 0)

    def take_cross():
        def one(half, carry):
            for g in range(8):
                i = half * 8 + g
                for b in range(BD_):
                    for v in range(4):
                        d0 = diag_b[i, b, pl.ds(2 * v, 8, stride=8), :]
                        d1 = diag_b[i, b, pl.ds(2 * v + 1, 8, stride=8), :]
                        value = cross_b[b, half, pl.ds(8 * v + g, 8, stride=32), :]
                        cterm[i, b, v] = value * jnp.sqrt(d0 * d1)
            return carry

        lax.fori_loop(0, 2, one, 0)

    def send_table():
        block = pl.multiple_of((me // 8) * 128, 128)
        turn = lax.rem(128 - lax.rem(me, 8) * 16, 128)
        lane = iota((32, 128), 1)
        tile = iota((32, 128), 0)

        def own(ref_rows):
            pair = []
            for route in range(2):
                row = jnp.broadcast_to(ref_rows(route, pl.ds(block, 128)), (32, 128))
                row = pltpu.roll(row, turn, axis=1)
                pair.append(pltpu.roll(row, 16, axis=1) if route else row)
            return jnp.where(lane < 16, pair[0], pair[1])

        routes = own(lambda route, cols: route_v[pl.ds(route, 1), cols])
        starts = [
            own(lambda route, cols, c=c: win_v[route, pl.ds(c, 1), cols]) for c in range(2)
        ]
        match = (routes == tile) & (lane < 32)
        low = butterfly(jnp.where(match, lane, 99), lane, 32, jnp.minimum)
        high = butterfly(jnp.where(match, lane, -1), lane, 32, jnp.maximum)
        table = jnp.zeros((32, 128), I32)
        for rank, chosen in enumerate((low, high)):
            picks = [
                butterfly(
                    jnp.where((lane == chosen) & (lane < 32), start, 0), lane, 32, jnp.add
                )
                for start in starts
            ]
            valid = (chosen >= 0) & (chosen < 32)
            granule = jnp.where(valid, chosen % 16, 0)
            first = [jnp.clip(pick // SP - 1, 0, FIRST_MAX) for pick in picks]
            for column, value in enumerate((granule, first[0] // 2, first[1])):
                table = jnp.where(lane == rank * 3 + column, value, table)
        tab_v[...] = table
        copy = pltpu.make_async_copy(tab_v, tab_s, tab_sem)
        copy.start()
        copy.wait()

    def weights(coord, ref):
        lane = iota((8, 512), 1)
        place = lane % 16
        match = []
        for route in range(2):
            row = jnp.broadcast_to(route_v[pl.ds(route, 1), :], (8, 512))
            match.append(row == me)
        low = jnp.minimum(
            jnp.where(match[0], place, 99), jnp.where(match[1], place + 16, 99)
        )
        high = jnp.maximum(
            jnp.where(match[0], place, -1), jnp.where(match[1], place + 16, -1)
        )
        low = butterfly(low, lane, 16, jnp.minimum)
        high = butterfly(high, lane, 16, jnp.maximum)
        total = jnp.sum(
            (match[0].astype(F32) + match[1].astype(F32))[0:1], axis=1, keepdims=True
        )
        for rank, chosen in enumerate((low, high)):
            live = (chosen < 32) if rank == 0 else (high != low) & (chosen >= 0)
            if True:
                pick = jnp.zeros((8, 512), I32)
                for route in range(2):
                    row = jnp.broadcast_to(win_v[route, pl.ds(coord, 1), :], (8, 512))
                    pick = pick + jnp.where(chosen == place + 16 * route, row, 0)
                pick = butterfly(pick, lane, 16, jnp.add)
                first = jnp.clip(pick // SP - 1, 0, FIRST_MAX)
                if coord == 0:
                    knot = (first // 2) * 2 + 2 * (place % 8) + place // 8
                else:
                    knot = first + place
                knot_f = knot.astype(F32)
                extra = jnp.where(
                    knot == 0, -1.0, jnp.where(knot == 63, 64.0, FAR)
                )
                start = pick.astype(F32) * (1.0 / SP)
                lead = start - knot_f
                lead_extra = start - extra

                def rows(block, carry, ref=ref, rank=rank, lead=lead, lead_extra=lead_extra,
                         live=live, coord=coord):
                    parts = []
                    for h in range(2):
                        pixel = (
                            iota((8, 512), 0) + (block * 16 + h * 8)
                        ).astype(F32) * (1.0 / SP)
                        d = jnp.abs(lead + pixel)
                        w = jnp.where(d <= 1.0, near_tap(d), far_tap(d))
                        w = jnp.where(d < 2.0, w, 0.0)
                        d2 = jnp.abs(lead_extra + pixel)
                        w = w + jnp.where(d2 < 2.0, far_tap(d2), 0.0)
                        if coord == 1:
                            w = jnp.where(live, w, 0.0)
                        parts.append(w)
                    ref[pl.ds(pl.multiple_of(block * 16, 16), 16), rank * 512 : rank * 512 + 512] = (
                        jnp.concatenate(parts, axis=0).astype(BF16)
                    )
                    return carry

                lax.fori_loop(0, PIX // 16, rows, 0)
        cover_v[...] = jnp.broadcast_to(1.0 / total, (8, 128))

    saves = [
        pltpu.make_async_copy(src, dst, out_sem.at[n])
        for n, (src, dst) in enumerate(
            ((roww, roww_h), (colt, colw_h), (cover_v, cover_h), (out_b, bal_h))
        )
    ]
    for sweep in range(SWEEPS):
        order = (1, 2) if sweep % 2 == 0 else (2, 1)
        disparity(0, sweep)
        if sweep == 0:
            loads[5].wait()
            take_coupling()
        elif sweep == 1:
            far_wait(1)
            far_signal(2)
            loads[9].wait()
            loads[10].wait()
            weights(0, roww)
            saves[0].start()
        else:
            weights(1, colw)
            colt[...] = colw[...].T
            saves[1].start()
            saves[2].start()
        for step, part in enumerate(order):
            take_responses(sweep, part - 1)
            if step == 0 and sweep < 2:
                far_wait(2 * sweep)
                far_signal(2 * sweep + 1)
            disparity(part, sweep)
        if sweep == 0:
            loads[6].wait()
            loads[7].wait()
            take_cross()
            loads[8].wait()
        solve(0, sweep)
        if sweep == 1:
            send_table()
        elif sweep == 2:
            far_wait(3)
        for part in order:
            take_grids(sweep, part - 1)
            solve(part, sweep)
    saves[3].start()

    lane8 = iota((8, 128), 1)
    lane_band = (lane8 % 64) // 16

    def fill(t):
        for rank in range(2):
            granule = tab_s[t, rank * 3]
            row = tab_s[t, rank * 3 + 1]
            column = tab_s[t, rank * 3 + 2]
            halves = []
            for c in range(2):
                value = None
                for b in range(BD_):
                    x = out_b[granule, b, pl.ds(2 * row + c, 8, stride=2), :]
                    x = pltpu.roll(x, lax.rem(b * 16 + 128 - column, 128), axis=1)
                    value = x if value is None else jnp.where(lane_band == b, x, value)
                halves.append(value)
            pay_out[t, rank * 16 : rank * 16 + 16, :] = jnp.concatenate(halves, axis=0).astype(BF16)

    def pay_copy(k):
        return pltpu.make_async_remote_copy(
            src_ref=pay_out.at[lax.rem(me + k, NG)],
            dst_ref=pay_in.at[me],
            send_sem=as_sem.at[k],
            recv_sem=ar_sem.at[k],
            device_id=(lax.rem(me + k, NG), mb),
            device_id_type=MESH,
        )

    def fill_and_send(n, carry):
        steps = [lax.rem(12 + n * 4 + u, NG) for u in range(4)]
        for k in steps:
            fill(lax.rem(me + k, NG))
        for k in steps:

            @pl.when(k > 0)
            def _(k=k):
                pay_copy(k).start()

        return carry

    lax.fori_loop(0, NG // 4, fill_and_send, 0)
    own_copy = pltpu.make_async_copy(pay_out.at[me], pay_in.at[me], own_sem)
    own_copy.start()
    own_copy.wait()

    def take_pay(k, carry):
        pltpu.make_async_remote_copy(
            src_ref=pay_out.at[lax.rem(me + k, NG)],
            dst_ref=pay_in.at[lax.rem(me + NG - k, NG)],
            send_sem=as_sem.at[k],
            recv_sem=ar_sem.at[k],
            device_id=(lax.rem(me + k, NG), mb),
            device_id_type=MESH,
        ).wait_recv()
        return carry

    lax.fori_loop(1, NG, take_pay, 0)

    for sweep in range(SWEEPS):
        for side in range(2):
            for piece in range(REACH + 1):
                halo_copy(sweep, side, piece).wait_send()
        for part in range(3):
            for k in range(1, NB):
                part_copy(sweep, part, k).wait_send()

    def sent_pay(k, carry):
        pay_copy(k).wait_send()
        return carry

    lax.fori_loop(1, NG, sent_pay, 0)
    for save in saves:
        save.wait()


def tile_kernel(
    pay_h,
    roww_h,
    colw_h,
    cover_h,
    pix_h,
    mid_h,
    bal_h,
    tile_h,
    pay_in,
    roww,
    colw,
    cover,
    pix_b,
    bal_b,
    tile_b,
    diagonal,
    rowpass,
    in_sem,
    out_sem,
):
    quarter = [pl.ds(4 * n, 4) for n in range(4)]
    pairs = [
        (pay_h, pay_in),
        (roww_h, roww),
        (colw_h, colw),
        (cover_h, cover),
        (pix_h, pix_b),
    ] + [(mid_h.at[part], bal_b.at[part]) for part in quarter]
    loads = [
        pltpu.make_async_copy(src, dst, in_sem.at[n]) for n, (src, dst) in enumerate(pairs)
    ]
    for load in loads:
        load.start()
    saves = [
        pltpu.make_async_copy(bal_b.at[part], bal_h.at[part], out_sem.at[n])
        for n, part in enumerate(quarter)
    ]

    def clear(n, carry):
        diagonal[n] = jnp.zeros((256, 256), BF16)
        return carry

    lax.fori_loop(0, 24, clear, 0)
    lane8 = iota((8, 128), 1)
    loads[0].wait()

    def expand(group, carry):
        rank = group // 2
        base = lax.rem(group, 2) * 16
        for s in range(16):
            block = pay_in[base + s, pl.ds(pl.multiple_of(rank * 16, 16), 16), :].astype(F32)
            for c in range(2):
                x = block[c * 8 : c * 8 + 8]
                for b in range(BD_):
                    parts = []
                    for parity in range(2):
                        turn = ((s % 8) * 16 - parity * 64 - b * 16) % 128
                        y = pltpu.roll(x, turn, axis=1) if turn else x
                        parts.append(jnp.where(lane8 // 16 == s % 8, y, 0.0))
                    diagonal[
                        group * 6 + b * 2 + c,
                        s * 16 : s * 16 + 16,
                        (s // 8) * 128 : (s // 8) * 128 + 128,
                    ] = jnp.concatenate(parts, axis=0).astype(BF16)
        return carry

    lax.fori_loop(0, 4, expand, 0)

    for load in loads[1:4]:
        load.wait()
    for load, save in zip(loads[5:], saves):
        load.wait()
        save.start()
    loads[4].wait()
    inverse_cover = cover[0:1, 0:1]

    def correct(b, carry):
        fields = []
        for c in range(2):
            for group in range(4):
                cols = slice(group * 256, group * 256 + 256)
                rowpass[:, cols] = dot(roww[:, cols], diagonal[group * 6 + b * 2 + c]).astype(BF16)
            fields.append(dot(rowpass[...], colw[...]))
        pixels = pix_b[b].astype(F32)
        value = pixels * (1.0 + fields[0] * inverse_cover) + fields[1] * inverse_cover
        tile_b[b] = value.astype(BF16)
        pltpu.make_async_copy(tile_b.at[b], tile_h.at[b], out_sem.at[4 + b]).start()
        return carry

    lax.fori_loop(0, BD_, correct, 0)
    for save in saves:
        save.wait()
    for b in range(BD_):
        pltpu.make_async_copy(tile_b.at[b], tile_h.at[b], out_sem.at[4 + b]).wait()


def per_device(
    prior_grids,
    pif_rhs,
    pif_diagonal,
    pif_cross,
    pif_coupling,
    neighbour_offset,
    neighbour_count,
    tile_route,
    tile_window,
    tile_pixels,
):
    def pairs(x):
        return x.reshape(GD, BD_, 2, 32, 128).transpose(0, 1, 3, 2, 4).reshape(GD, BD_, 64, 128)

    prior = pairs(prior_grids)
    rhs = pairs(pif_rhs)
    diag = pairs(pif_diagonal)
    cross = (
        pif_cross.reshape(2, 8, BD_, 32, 128).transpose(2, 0, 3, 1, 4).reshape(BD_, 2, 256, 128)
    )
    coupling = (
        pif_coupling.reshape(GD, SLOTS, BD_, 32, 128)
        .transpose(0, 2, 3, 1, 4)
        .reshape(GD, BD_, 256, 128)
    )
    any_ = pl.BlockSpec(memory_space=pl.ANY)
    dma = pltpu.SemaphoreType.DMA
    middle, payload, roww, colw, cover = pl.pallas_call(
        kernel,
        out_shape=(
            jax.ShapeDtypeStruct((GD, BD_, 64, 128), F32),
            jax.ShapeDtypeStruct((NG, 32, 128), BF16),
            jax.ShapeDtypeStruct((PIX, 1024), BF16),
            jax.ShapeDtypeStruct((1024, PIX), BF16),
            jax.ShapeDtypeStruct((8, 128), F32),
        ),
        in_specs=[any_] * 9,
        out_specs=(any_,) * 5,
        scratch_shapes=[
            pltpu.SMEM((SLOTS, GD), I32),
            pltpu.SMEM((GD,), I32),
            pltpu.VMEM((2, NG * GD), I32),
            pltpu.VMEM((2, 2, NG * GD), I32),
            pltpu.VMEM((GD, BD_, 64, 128), F32),
            pltpu.VMEM((GD, BD_, 64, 128), F32),
            pltpu.VMEM((GD, BD_, 64, 128), F32),
            pltpu.VMEM((BD_, 2, 256, 128), F32),
            pltpu.VMEM((GD, BD_, 256, 128), BF16),
            pltpu.VMEM((GD, BD_, 64, 128), F32),
            pltpu.VMEM((2, GD + 2 * REACH, BD_, 2, 4, 8, 128), F32),
            pltpu.VMEM((GD + 2 * REACH, BD_, 4, 8, 128), F32),
            pltpu.VMEM((GD, BD_, SLOTS, 4, 8, 128), F32),
            pltpu.VMEM((GD, BD_, 4, 8, 128), F32),
            pltpu.VMEM((512, 128), F32),
            pltpu.VMEM((512, 128), F32),
            pltpu.VMEM((3, 32, 128), F32),
            pltpu.VMEM((SWEEPS, 2, 2, REACH, BD_, 32, 128), BF16),
            pltpu.VMEM((SWEEPS, 2, 2, REACH, BD_, 32, 128), BF16),
            pltpu.VMEM((SWEEPS, 3, 32, 128), BF16),
            pltpu.VMEM((SWEEPS, 3, NB - 1, 32, 128), BF16),
            pltpu.VMEM((NG, 128), I32),
            pltpu.SMEM((NG, 128), I32),
            pltpu.VMEM((NG, 32, 128), BF16),
            pltpu.VMEM((PIX, 1024), BF16),
            pltpu.VMEM((PIX, 1024), BF16),
            pltpu.VMEM((1024, PIX), BF16),
            pltpu.VMEM((8, 128), F32),
            dma((11,)),
            dma((4,)),
            dma((SWEEPS, 2, REACH + 1)),
            dma((SWEEPS, 2, REACH + 1)),
            dma((SWEEPS, 3, NB - 1)),
            dma((SWEEPS, 3, NB - 1)),
            dma((NG,)),
            dma((NG,)),
            dma,
            dma,
            pltpu.SemaphoreType.REGULAR((FAR_STEPS, 2)),
        ],
        compiler_params=pltpu.CompilerParams(
            collective_id=0, has_side_effects=True, vmem_limit_bytes=60 * 1024 * 1024
        ),
        name="balance",
    )(
        neighbour_offset.T,
        neighbour_count,
        prior,
        rhs,
        diag,
        cross,
        coupling,
        tile_route.T,
        tile_window.transpose(1, 2, 0),
    )
    balanced, tiles = pl.pallas_call(
        tile_kernel,
        out_shape=(
            jax.ShapeDtypeStruct((GD, BD_, 64, 128), F32),
            jax.ShapeDtypeStruct((BD_, PIX, PIX), BF16),
        ),
        in_specs=[any_] * 6,
        out_specs=(any_, any_),
        scratch_shapes=[
            pltpu.VMEM((NG, 32, 128), BF16),
            pltpu.VMEM((PIX, 1024), BF16),
            pltpu.VMEM((1024, PIX), BF16),
            pltpu.VMEM((8, 128), F32),
            pltpu.VMEM((BD_, PIX, PIX), BF16),
            pltpu.VMEM((GD, BD_, 64, 128), F32),
            pltpu.VMEM((BD_, PIX, PIX), BF16),
            pltpu.VMEM((24, 256, 256), BF16),
            pltpu.VMEM((PIX, 1024), BF16),
            dma((9,)),
            dma((7,)),
        ],
        compiler_params=pltpu.CompilerParams(vmem_limit_bytes=TILE_VMEM),
        name="tiles",
    )(payload, roww, colw, cover, tile_pixels[0], middle)
    balanced = (
        balanced.reshape(GD, BD_, 32, 2, 128)
        .transpose(0, 1, 3, 2, 4)
        .reshape(GD, BD_, 2, 4096)
    )
    return (balanced, tiles[None])


def solution(mesh):
    placed = (
        P("gran", "band", None, None),
        P("gran", "band", None, None),
        P("gran", "band", None, None),
        P("gran", "band", None),
        P("gran", None, "band", None),
        P("gran", None),
        P("gran"),
        P(),
        P(),
        P("gran", "band", None, None),
    )
    return jax.shard_map(
        per_device,
        mesh=mesh,
        in_specs=placed,
        out_specs=(P("gran", "band", None, None), P("gran", "band", None, None)),
        check_vma=False,
    )
```

```python
import jax
import jax.numpy as jnp
from jax import lax
from jax.experimental import pallas as pl
from jax.experimental.pallas import tpu as pltpu
from jax.sharding import PartitionSpec as P

MESH = pl.DeviceIdType.MESH
F32 = jnp.float32
BF16 = jnp.bfloat16
I32 = jnp.int32

BANDS = 12
PATCH = 8
REACH = 4
SWEEPS = 3
SP = 32
ROBUST = 0.3 * BANDS * PATCH * PATCH

GD = 16
BD_ = 3
NG = 32
NB = 4
SLOTS = 8
PIX = 256
WIN = 16
FIRST_MAX = 64 - WIN
FAR = 1000.0
FAR_STEPS = 4
TILE_VMEM = 14 * 1024 * 1024


def iota(shape, dim):
    return lax.broadcasted_iota(I32, shape, dim)


def dot(a, b):
    return jnp.dot(a, b, preferred_element_type=F32)


def butterfly(x, lane, width, op):
    size = x.shape[1]
    step = 1
    while step < width:
        other = jnp.where(
            (lane // step) % 2 == 0,
            pltpu.roll(x, size - step, axis=1),
            pltpu.roll(x, step, axis=1),
        )
        x = op(x, other)
        step *= 2
    return x


def far_tap(d):
    return ((-0.5 * d + 2.5) * d - 4.0) * d + 2.0


def near_tap(d):
    return (1.5 * d - 2.5) * d * d + 1.0


PARTS = ((4, 8), (0, 4), (12, 4))


def packing(part):
    count = PARTS[part][1]
    blocks = 16 // count
    return count, blocks, 64 // blocks


def kernel(
    off_h,
    cnt_h,
    prior_h,
    rhs_h,
    diag_h,
    cross_h,
    coup_h,
    route_h,
    win_h,
    bal_h,
    pay_in,
    roww_h,
    colw_h,
    cover_h,
    off_s,
    cnt_s,
    route_v,
    win_v,
    prior_b,
    rhs_b,
    diag_b,
    cross_b,
    coup_b,
    out_b,
    grids,
    resp,
    coup,
    cterm,
    disp,
    spread,
    weight,
    halo_out,
    halo_in,
    part_out,
    part_in,
    tab_v,
    tab_s,
    pay_out,
    roww,
    colw,
    colt,
    cover_v,
    in_sem,
    out_sem,
    hs_sem,
    hr_sem,
    ps_sem,
    pr_sem,
    as_sem,
    ar_sem,
    tab_sem,
    own_sem,
    far_sem,
):
    me = lax.axis_index("gran")
    mb = lax.axis_index("band")
    right = lax.rem(me + 1, NG)
    left = lax.rem(me + NG - 1, NG)

    barrier = pltpu.get_barrier_semaphore()
    for other in (left, right):
        pl.semaphore_signal(barrier, inc=1, device_id=(other, mb), device_id_type=MESH)
    for k in range(1, NB):
        pl.semaphore_signal(
            barrier, inc=1, device_id=(me, lax.rem(mb + k, NB)), device_id_type=MESH
        )

    def far_signal(step):
        distance = 1 << step
        for side, shift in enumerate((distance, NG - distance)):
            pl.semaphore_signal(
                far_sem.at[step, side],
                inc=1,
                device_id=(lax.rem(me + shift, NG), mb),
                device_id_type=MESH,
            )

    def far_wait(step):
        for side in range(2):
            pl.semaphore_wait(far_sem.at[step, side], 1)

    ends = (pl.ds(0, REACH), pl.ds(GD - REACH, REACH))
    middle = pl.ds(REACH, GD - 2 * REACH)
    pairs = [(prior_h.at[part], prior_b.at[part]) for part in (*ends, middle)]
    pairs += [
        (off_h, off_s),
        (cnt_h, cnt_s),
        (coup_h, coup_b),
        (diag_h, diag_b),
        (cross_h, cross_b),
        (rhs_h, rhs_b),
        (route_h, route_v),
        (win_h, win_v),
    ]
    loads = [
        pltpu.make_async_copy(src, dst, in_sem.at[n]) for n, (src, dst) in enumerate(pairs)
    ]
    for load in loads[:2]:
        load.start()

    lane128 = iota((128, 128), 1)
    sub128 = iota((128, 128), 0)
    gather_table = ((sub128 % 64) // 8 == lane128 % 8).astype(F32).astype(BF16)
    spread_table = ((lane128 % 64) // 8 == sub128 % 8).astype(F32).astype(BF16)

    def take_prior(i):
        for b in range(BD_):
            for v in range(4):
                g0 = prior_b[i, b, pl.ds(2 * v, 8, stride=8), :]
                g1 = prior_b[i, b, pl.ds(2 * v + 1, 8, stride=8), :]
                grids[0, REACH + i, b, 0, v] = g0
                grids[0, REACH + i, b, 1, v] = g1
                resp[REACH + i, b, v] = g0 + g1

    def halo_rows(sweep, side, e, i):
        for b in range(BD_):
            halo_out[sweep, side, 0, e, b] = resp[REACH + i, b].reshape(32, 128).astype(BF16)
            halo_out[sweep, side, 1, e, b] = (
                grids[sweep % 2, REACH + i, b, 0].reshape(32, 128).astype(BF16)
            )

    for load in loads[:2]:
        load.wait()
    for load in loads[2:]:
        load.start()
    for side, base in ((1, 0), (0, GD - REACH)):

        def first_halo(e, carry, side=side, base=base):
            take_prior(base + e)
            halo_rows(0, side, e, base + e)
            return carry

        lax.fori_loop(0, REACH, first_halo, 0)

    pl.semaphore_wait(barrier, 2 + NB - 1)

    def halo_copy(sweep, side, piece):
        whole = not isinstance(piece, jax.Array) and piece == REACH
        part = (sweep, side, 1) if whole else (sweep, side, 0, piece)
        return pltpu.make_async_remote_copy(
            src_ref=halo_out.at[part],
            dst_ref=halo_in.at[part],
            send_sem=hs_sem.at[sweep, side, piece],
            recv_sem=hr_sem.at[sweep, side, piece],
            device_id=(right if side == 0 else left, mb),
            device_id_type=MESH,
        )

    def part_copy(sweep, part, k):
        return pltpu.make_async_remote_copy(
            src_ref=part_out.at[sweep, part, pl.ds(0, packing(part)[2])],
            dst_ref=part_in.at[sweep, part, k - 1, pl.ds(0, packing(part)[2])],
            send_sem=ps_sem.at[sweep, part, k - 1],
            recv_sem=pr_sem.at[sweep, part, k - 1],
            device_id=(me, lax.rem(mb + k, NB)),
            device_id_type=MESH,
        )

    for piece in range(REACH + 1):
        for side in range(2):
            halo_copy(0, side, piece).start()
    far_signal(0)

    for load in loads[2:5]:
        load.wait()

    def rest(k, carry):
        take_prior(REACH + k)
        return carry

    lax.fori_loop(0, GD - 2 * REACH, rest, 0)

    for part in range(3):
        count, blocks, rows = packing(part)
        lane_block = iota((rows, 128), 1) // 8
        slot = (lane_block // count) * (SLOTS // blocks) + iota((rows, 128), 0) // 8
        counts = jnp.zeros((rows, 128), I32)
        for k in range(count):
            counts = jnp.where(lane_block % count == k, cnt_s[PARTS[part][0] + k], counts)
        weight[part, :rows] = (slot < counts).astype(F32)

    def disparity(part, sweep):
        base = PARTS[part][0]
        count, blocks, height = packing(part)

        def one(k, carry):
            i = base + k
            own = [resp[REACH + i, b] for b in range(BD_)]
            for s in range(SLOTS):
                n = REACH + i + off_s[s, i]
                total = None
                for b in range(BD_):
                    diff = own[b] - resp[n, b]
                    square = diff * diff
                    total = square if total is None else total + square
                disp[pl.ds(pl.multiple_of(k * 64 + s * 8, 8), 8), :] = (
                    total[0] + total[1] + total[2] + total[3]
                )
            return carry

        lax.fori_loop(0, count, one, 0)
        sums = dot(disp[: count * 64].astype(BF16), gather_table)
        packed = jnp.zeros((height, 128), F32)
        lane_block = iota((height, 128), 1) // 8
        for k in range(count):
            for h in range(blocks):
                at = k * 64 + h * height
                packed = jnp.where(lane_block == h * count + k, sums[at : at + height], packed)
        part_out[sweep, part, :height] = packed.astype(BF16)
        for k in (2, 1, 3):
            part_copy(sweep, part, k).start()

    def solve(part, sweep):
        base = PARTS[part][0]
        count, blocks, height = packing(part)
        now, later = sweep % 2, (sweep + 1) % 2
        last = sweep == SWEEPS - 1
        for k in range(1, NB):
            part_copy(sweep, part, k).wait_recv()
        total = part_out[sweep, part, :height].astype(F32)
        for k in range(NB - 1):
            total = total + part_in[sweep, part, k, :height].astype(F32)
        robust = weight[part, :height] / (1.0 + total * (1.0 / ROBUST))
        lane_block = iota((height, 128), 1) // 8
        rows = []
        for k in range(count):
            for h in range(blocks):
                rows.append(jnp.where(lane_block == h * count + k, robust, 0.0))
        spread[: count * 64] = dot(jnp.concatenate(rows, axis=0).astype(BF16), spread_table)

        def one(k, carry):
            i = base + k
            places = [REACH + i + off_s[s, i] for s in range(SLOTS)]
            for b in range(BD_):
                sigma = drive0 = drive1 = None
                for s in range(SLOTS):
                    rob = spread[pl.ds(pl.multiple_of(k * 64 + s * 8, 8), 8), :]
                    eff = rob[None] * coup[i, b, s]
                    add0 = eff * grids[now, places[s], b, 0]
                    add1 = eff * grids[now, places[s], b, 1]
                    if s == 0:
                        sigma, drive0, drive1 = eff, add0, add1
                    else:
                        sigma, drive0, drive1 = sigma + eff, drive0 + add0, drive1 + add1
                for v in range(4):
                    even = pl.ds(2 * v, 8, stride=8)
                    odd = pl.ds(2 * v + 1, 8, stride=8)
                    r0 = rhs_b[i, b, even, :] + drive0[v]
                    r1 = rhs_b[i, b, odd, :] + drive1[v]
                    first = diag_b[i, b, even, :] + sigma[v]
                    second = diag_b[i, b, odd, :] + sigma[v]
                    cross = cterm[i, b, v]
                    inverse = 1.0 / (first * second - cross * cross)
                    g0 = (second * r0 - cross * r1) * inverse
                    g1 = (first * r1 - cross * r0) * inverse
                    if last:
                        out_b[i, b, even, :] = g0
                        out_b[i, b, odd, :] = g1
                    else:
                        grids[later, REACH + i, b, 0, v] = g0
                        grids[later, REACH + i, b, 1, v] = g1
                        resp[REACH + i, b, v] = g0 + g1
            if part > 0 and not last:
                halo_rows(sweep + 1, 2 - part, k, i)
                halo_copy(sweep + 1, 2 - part, k).start()
            return carry

        lax.fori_loop(0, count, one, 0)
        if part > 0 and not last:
            halo_copy(sweep + 1, 2 - part, REACH).start()

    def take_responses(sweep, side):
        def one(e, carry):
            halo_copy(sweep, side, e).wait_recv()
            for b in range(BD_):
                value = halo_in[sweep, side, 0, e, b].astype(F32)
                resp[e + side * (REACH + GD), b] = value.reshape(4, 8, 128)
            return carry

        lax.fori_loop(0, REACH, one, 0)

    def take_grids(sweep, side):
        now = sweep % 2
        halo_copy(sweep, side, REACH).wait_recv()

        def one(e, carry):
            place = e + side * (REACH + GD)
            for b in range(BD_):
                g0 = halo_in[sweep, side, 1, e, b].astype(F32).reshape(4, 8, 128)
                grids[now, place, b, 0] = g0
                grids[now, place, b, 1] = resp[place, b] - g0
            return carry

        lax.fori_loop(0, REACH, one, 0)

    def take_coupling():
        row = iota((256, 256), 0)
        source = (4 * (row % 8) + (row // 8) % 4) * 8 + row // 32
        order = (iota((256, 256), 1) == source).astype(F32).astype(BF16)

        def one(i, carry):
            for b in range(BD_):
                both = jnp.concatenate([coup_b[i, b], coup_b[i + 8, b]], axis=1)
                moved = dot(order, both)
                coup[i, b] = moved[:, :128].reshape(SLOTS, 4, 8, 128)
                coup[i + 8, b] = moved[:, 128:].reshape(SLOTS, 4, 8, 128)
            return carry

        lax.fori_loop(0, GD // 2, one, 0)

    def take_cross():
        def one(half, carry):
            for g in range(8):
                i = half * 8 + g
                for b in range(BD_):
                    for v in range(4):
                        d0 = diag_b[i, b, pl.ds(2 * v, 8, stride=8), :]
                        d1 = diag_b[i, b, pl.ds(2 * v + 1, 8, stride=8), :]
                        value = cross_b[b, half, pl.ds(8 * v + g, 8, stride=32), :]
                        cterm[i, b, v] = value * jnp.sqrt(d0 * d1)
            return carry

        lax.fori_loop(0, 2, one, 0)

    def send_table():
        block = pl.multiple_of((me // 8) * 128, 128)
        turn = lax.rem(128 - lax.rem(me, 8) * 16, 128)
        lane = iota((32, 128), 1)
        tile = iota((32, 128), 0)

        def own(ref_rows):
            pair = []
            for route in range(2):
                row = jnp.broadcast_to(ref_rows(route, pl.ds(block, 128)), (32, 128))
                row = pltpu.roll(row, turn, axis=1)
                pair.append(pltpu.roll(row, 16, axis=1) if route else row)
            return jnp.where(lane < 16, pair[0], pair[1])

        routes = own(lambda route, cols: route_v[pl.ds(route, 1), cols])
        starts = [
            own(lambda route, cols, c=c: win_v[route, pl.ds(c, 1), cols]) for c in range(2)
        ]
        match = (routes == tile) & (lane < 32)
        low = butterfly(jnp.where(match, lane, 99), lane, 32, jnp.minimum)
        high = butterfly(jnp.where(match, lane, -1), lane, 32, jnp.maximum)
        table = jnp.zeros((32, 128), I32)
        for rank, chosen in enumerate((low, high)):
            picks = [
                butterfly(
                    jnp.where((lane == chosen) & (lane < 32), start, 0), lane, 32, jnp.add
                )
                for start in starts
            ]
            valid = (chosen >= 0) & (chosen < 32)
            granule = jnp.where(valid, chosen % 16, 0)
            first = [jnp.clip(pick // SP - 1, 0, FIRST_MAX) for pick in picks]
            turns = [(b * 16 + 128 - first[1]) % 128 for b in range(BD_)]
            for column, value in enumerate((granule, (first[0] // 2) * 2, *turns)):
                table = jnp.where(lane == rank * 5 + column, value, table)
        tab_v[...] = table
        copy = pltpu.make_async_copy(tab_v, tab_s, tab_sem)
        copy.start()
        copy.wait()

    def weights(coord, ref):
        lane = iota((8, 512), 1)
        place = lane % 16
        match = []
        for route in range(2):
            row = jnp.broadcast_to(route_v[pl.ds(route, 1), :], (8, 512))
            match.append(row == me)
        low = jnp.minimum(
            jnp.where(match[0], place, 99), jnp.where(match[1], place + 16, 99)
        )
        high = jnp.maximum(
            jnp.where(match[0], place, -1), jnp.where(match[1], place + 16, -1)
        )
        low = butterfly(low, lane, 16, jnp.minimum)
        high = butterfly(high, lane, 16, jnp.maximum)
        total = jnp.sum(
            (match[0].astype(F32) + match[1].astype(F32))[0:1], axis=1, keepdims=True
        )
        for rank, chosen in enumerate((low, high)):
            live = (chosen < 32) if rank == 0 else (high != low) & (chosen >= 0)
            if True:
                pick = jnp.zeros((8, 512), I32)
                for route in range(2):
                    row = jnp.broadcast_to(win_v[route, pl.ds(coord, 1), :], (8, 512))
                    pick = pick + jnp.where(chosen == place + 16 * route, row, 0)
                pick = butterfly(pick, lane, 16, jnp.add)
                first = jnp.clip(pick // SP - 1, 0, FIRST_MAX)
                if coord == 0:
                    knot = (first // 2) * 2 + 2 * (place % 8) + place // 8
                else:
                    knot = first + place
                knot_f = knot.astype(F32)
                extra = jnp.where(
                    knot == 0, -1.0, jnp.where(knot == 63, 64.0, FAR)
                )
                start = pick.astype(F32) * (1.0 / SP)
                lead = start - knot_f
                lead_extra = start - extra

                def rows(block, carry, ref=ref, rank=rank, lead=lead, lead_extra=lead_extra,
                         live=live, coord=coord):
                    parts = []
                    for h in range(2):
                        pixel = (
                            iota((8, 512), 0) + (block * 16 + h * 8)
                        ).astype(F32) * (1.0 / SP)
                        d = jnp.abs(lead + pixel)
                        w = jnp.where(d <= 1.0, near_tap(d), far_tap(d))
                        w = jnp.where(d < 2.0, w, 0.0)
                        d2 = jnp.abs(lead_extra + pixel)
                        w = w + jnp.where(d2 < 2.0, far_tap(d2), 0.0)
                        if coord == 1:
                            w = jnp.where(live, w, 0.0)
                        parts.append(w)
                    ref[pl.ds(pl.multiple_of(block * 16, 16), 16), rank * 512 : rank * 512 + 512] = (
                        jnp.concatenate(parts, axis=0).astype(BF16)
                    )
                    return carry

                lax.fori_loop(0, PIX // 16, rows, 0)
        cover_v[...] = jnp.broadcast_to(1.0 / total, (8, 128))

    saves = [
        pltpu.make_async_copy(src, dst, out_sem.at[n])
        for n, (src, dst) in enumerate(
            ((roww, roww_h), (colt, colw_h), (cover_v, cover_h), (out_b, bal_h))
        )
    ]
    for sweep in range(SWEEPS):
        order = (1, 2) if sweep % 2 == 0 else (2, 1)
        disparity(0, sweep)
        if sweep == 0:
            loads[5].wait()
            take_coupling()
        elif sweep == 1:
            far_wait(1)
            far_signal(2)
            loads[9].wait()
            loads[10].wait()
            weights(0, roww)
            saves[0].start()
        else:
            weights(1, colw)
            colt[...] = colw[...].T
            saves[1].start()
            saves[2].start()
        for step, part in enumerate(order):
            take_responses(sweep, part - 1)
            if step == 0 and sweep < 2:
                far_wait(2 * sweep)
                far_signal(2 * sweep + 1)
            disparity(part, sweep)
        if sweep == 0:
            loads[6].wait()
            loads[7].wait()
            take_cross()
            loads[8].wait()
        solve(0, sweep)
        if sweep == 1:
            send_table()
        elif sweep == 2:
            far_wait(3)
        for part in order:
            take_grids(sweep, part - 1)
            solve(part, sweep)
    saves[3].start()

    lane8 = iota((8, 128), 1)
    lane_band = (lane8 % 64) // 16

    def fill(t):
        for rank in range(2):
            granule = tab_s[t, rank * 5]
            row = tab_s[t, rank * 5 + 1]
            halves = []
            for c in range(2):
                value = None
                for b in range(BD_):
                    x = out_b[granule, b, pl.ds(row + c, 8, stride=2), :]
                    x = pltpu.roll(x, tab_s[t, rank * 5 + 2 + b], axis=1)
                    value = x if value is None else jnp.where(lane_band == b, x, value)
                halves.append(value)
            pay_out[t, rank * 16 : rank * 16 + 16, :] = jnp.concatenate(halves, axis=0).astype(BF16)

    def pay_copy(k):
        return pltpu.make_async_remote_copy(
            src_ref=pay_out.at[lax.rem(me + k, NG)],
            dst_ref=pay_in.at[me],
            send_sem=as_sem.at[k],
            recv_sem=ar_sem.at[k],
            device_id=(lax.rem(me + k, NG), mb),
            device_id_type=MESH,
        )

    def fill_and_send(n, carry):
        steps = [lax.rem(12 + n * 4 + u, NG) for u in range(4)]
        for k in steps:
            fill(lax.rem(me + k, NG))
        for k in steps:

            @pl.when(k > 0)
            def _(k=k):
                pay_copy(k).start()

        return carry

    lax.fori_loop(0, NG // 4, fill_and_send, 0)
    own_copy = pltpu.make_async_copy(pay_out.at[me], pay_in.at[me], own_sem)
    own_copy.start()
    own_copy.wait()
    for sweep in range(SWEEPS):
        for side in range(2):
            for piece in range(REACH + 1):
                halo_copy(sweep, side, piece).wait_send()
        for part in range(3):
            for k in range(1, NB):
                part_copy(sweep, part, k).wait_send()
    for save in saves:
        save.wait()

    def take_pay(k, carry):
        pltpu.make_async_remote_copy(
            src_ref=pay_out.at[lax.rem(me + k, NG)],
            dst_ref=pay_in.at[lax.rem(me + NG - k, NG)],
            send_sem=as_sem.at[k],
            recv_sem=ar_sem.at[k],
            device_id=(lax.rem(me + k, NG), mb),
            device_id_type=MESH,
        ).wait_recv()
        return carry

    lax.fori_loop(1, NG, take_pay, 0)

    def sent_pay(k, carry):
        pay_copy(k).wait_send()
        return carry

    lax.fori_loop(1, NG, sent_pay, 0)


def tile_kernel(
    pay_h,
    roww_h,
    colw_h,
    cover_h,
    pix_h,
    mid_h,
    bal_h,
    tile_h,
    pay_in,
    roww,
    colw,
    cover,
    pix_b,
    bal_b,
    tile_b,
    diagonal,
    rowpass,
    in_sem,
    out_sem,
):
    quarter = [pl.ds(4 * n, 4) for n in range(4)]
    pairs = [
        (pay_h, pay_in),
        (roww_h, roww),
        (colw_h, colw),
        (cover_h, cover),
        (pix_h, pix_b),
    ] + [(mid_h.at[part], bal_b.at[part]) for part in quarter]
    loads = [
        pltpu.make_async_copy(src, dst, in_sem.at[n]) for n, (src, dst) in enumerate(pairs)
    ]
    for load in loads:
        load.start()
    saves = [
        pltpu.make_async_copy(bal_b.at[part], bal_h.at[part], out_sem.at[n])
        for n, part in enumerate(quarter)
    ]

    def clear(n, carry):
        diagonal[n] = jnp.zeros((256, 256), BF16)
        return carry

    lax.fori_loop(0, 24, clear, 0)
    lane8 = iota((8, 128), 1)
    loads[0].wait()

    def expand(b):
        for group in range(4):
            rank, base = group // 2, (group % 2) * 16
            for s in range(16):
                block = pay_in[base + s, rank * 16 : rank * 16 + 16, :].astype(F32)
                for c in range(2):
                    parts = []
                    for parity in range(2):
                        turn = ((s % 8) * 16 - parity * 64 - b * 16) % 128
                        y = block[c * 8 : c * 8 + 8]
                        y = pltpu.roll(y, turn, axis=1) if turn else y
                        parts.append(jnp.where(lane8 // 16 == s % 8, y, 0.0))
                    diagonal[
                        group * 6 + b * 2 + c,
                        s * 16 : s * 16 + 16,
                        (s // 8) * 128 : (s // 8) * 128 + 128,
                    ] = jnp.concatenate(parts, axis=0).astype(BF16)

    expand(0)
    for load in loads[1:4]:
        load.wait()
    for load, save in zip(loads[5:], saves):
        load.wait()
        save.start()
    loads[4].wait()
    inverse_cover = cover[0:1, 0:1]

    for b in range(BD_):
        if b + 1 < BD_:
            expand(b + 1)
        fields = []
        for c in range(2):
            for group in range(4):
                cols = slice(group * 256, group * 256 + 256)
                rowpass[:, cols] = dot(roww[:, cols], diagonal[group * 6 + b * 2 + c]).astype(BF16)
            fields.append(dot(rowpass[...], colw[...]))
        pixels = pix_b[b].astype(F32)
        value = pixels * (1.0 + fields[0] * inverse_cover) + fields[1] * inverse_cover
        tile_b[b] = value.astype(BF16)
        pltpu.make_async_copy(tile_b.at[b], tile_h.at[b], out_sem.at[4 + b]).start()

    for save in saves:
        save.wait()
    for b in range(BD_):
        pltpu.make_async_copy(tile_b.at[b], tile_h.at[b], out_sem.at[4 + b]).wait()


def per_device(
    prior_grids,
    pif_rhs,
    pif_diagonal,
    pif_cross,
    pif_coupling,
    neighbour_offset,
    neighbour_count,
    tile_route,
    tile_window,
    tile_pixels,
):
    def pairs(x):
        return x.reshape(GD, BD_, 2, 32, 128).transpose(0, 1, 3, 2, 4).reshape(GD, BD_, 64, 128)

    prior = pairs(prior_grids)
    rhs = pairs(pif_rhs)
    diag = pairs(pif_diagonal)
    cross = (
        pif_cross.reshape(2, 8, BD_, 32, 128).transpose(2, 0, 3, 1, 4).reshape(BD_, 2, 256, 128)
    )
    coupling = (
        pif_coupling.reshape(GD, SLOTS, BD_, 32, 128)
        .transpose(0, 2, 3, 1, 4)
        .reshape(GD, BD_, 256, 128)
    )
    any_ = pl.BlockSpec(memory_space=pl.ANY)
    hbm = pl.BlockSpec(memory_space=pltpu.HBM)
    dma = pltpu.SemaphoreType.DMA
    middle, payload, roww, colw, cover = pl.pallas_call(
        kernel,
        out_shape=(
            jax.ShapeDtypeStruct((GD, BD_, 64, 128), F32),
            jax.ShapeDtypeStruct((NG, 32, 128), BF16),
            jax.ShapeDtypeStruct((PIX, 1024), BF16),
            jax.ShapeDtypeStruct((1024, PIX), BF16),
            jax.ShapeDtypeStruct((8, 128), F32),
        ),
        in_specs=[hbm] * 9,
        out_specs=(any_,) * 5,
        scratch_shapes=[
            pltpu.SMEM((SLOTS, GD), I32),
            pltpu.SMEM((GD,), I32),
            pltpu.VMEM((2, NG * GD), I32),
            pltpu.VMEM((2, 2, NG * GD), I32),
            pltpu.VMEM((GD, BD_, 64, 128), F32),
            pltpu.VMEM((GD, BD_, 64, 128), F32),
            pltpu.VMEM((GD, BD_, 64, 128), F32),
            pltpu.VMEM((BD_, 2, 256, 128), F32),
            pltpu.VMEM((GD, BD_, 256, 128), BF16),
            pltpu.VMEM((GD, BD_, 64, 128), F32),
            pltpu.VMEM((2, GD + 2 * REACH, BD_, 2, 4, 8, 128), F32),
            pltpu.VMEM((GD + 2 * REACH, BD_, 4, 8, 128), F32),
            pltpu.VMEM((GD, BD_, SLOTS, 4, 8, 128), F32),
            pltpu.VMEM((GD, BD_, 4, 8, 128), F32),
            pltpu.VMEM((512, 128), F32),
            pltpu.VMEM((512, 128), F32),
            pltpu.VMEM((3, 32, 128), F32),
            pltpu.VMEM((SWEEPS, 2, 2, REACH, BD_, 32, 128), BF16),
            pltpu.VMEM((SWEEPS, 2, 2, REACH, BD_, 32, 128), BF16),
            pltpu.VMEM((SWEEPS, 3, 32, 128), BF16),
            pltpu.VMEM((SWEEPS, 3, NB - 1, 32, 128), BF16),
            pltpu.VMEM((NG, 128), I32),
            pltpu.SMEM((NG, 128), I32),
            pltpu.VMEM((NG, 32, 128), BF16),
            pltpu.VMEM((PIX, 1024), BF16),
            pltpu.VMEM((PIX, 1024), BF16),
            pltpu.VMEM((1024, PIX), BF16),
            pltpu.VMEM((8, 128), F32),
            dma((11,)),
            dma((4,)),
            dma((SWEEPS, 2, REACH + 1)),
            dma((SWEEPS, 2, REACH + 1)),
            dma((SWEEPS, 3, NB - 1)),
            dma((SWEEPS, 3, NB - 1)),
            dma((NG,)),
            dma((NG,)),
            dma,
            dma,
            pltpu.SemaphoreType.REGULAR((FAR_STEPS, 2)),
        ],
        compiler_params=pltpu.CompilerParams(
            collective_id=0, has_side_effects=True, vmem_limit_bytes=36 * 1024 * 1024
        ),
        name="balance",
    )(
        *(
            pltpu.with_memory_space_constraint(x, pltpu.HBM)
            for x in (
                neighbour_offset.T,
                neighbour_count,
                prior,
                rhs,
                diag,
                cross,
                coupling,
                tile_route.T,
                tile_window.transpose(1, 2, 0),
            )
        )
    )
    balanced, tiles = pl.pallas_call(
        tile_kernel,
        out_shape=(
            jax.ShapeDtypeStruct((GD, BD_, 64, 128), F32),
            jax.ShapeDtypeStruct((BD_, PIX, PIX), BF16),
        ),
        in_specs=[any_] * 6,
        out_specs=(any_, any_),
        scratch_shapes=[
            pltpu.VMEM((NG, 32, 128), BF16),
            pltpu.VMEM((PIX, 1024), BF16),
            pltpu.VMEM((1024, PIX), BF16),
            pltpu.VMEM((8, 128), F32),
            pltpu.VMEM((BD_, PIX, PIX), BF16),
            pltpu.VMEM((GD, BD_, 64, 128), F32),
            pltpu.VMEM((BD_, PIX, PIX), BF16),
            pltpu.VMEM((24, 256, 256), BF16),
            pltpu.VMEM((PIX, 1024), BF16),
            dma((9,)),
            dma((7,)),
        ],
        compiler_params=pltpu.CompilerParams(vmem_limit_bytes=TILE_VMEM),
        name="tiles",
    )(payload, roww, colw, cover, tile_pixels[0], middle)
    balanced = (
        balanced.reshape(GD, BD_, 32, 2, 128)
        .transpose(0, 1, 3, 2, 4)
        .reshape(GD, BD_, 2, 4096)
    )
    return (balanced, tiles[None])


def solution(mesh):
    placed = (
        P("gran", "band", None, None),
        P("gran", "band", None, None),
        P("gran", "band", None, None),
        P("gran", "band", None),
        P("gran", None, "band", None),
        P("gran", None),
        P("gran"),
        P(),
        P(),
        P("gran", "band", None, None),
    )
    return jax.shard_map(
        per_device,
        mesh=mesh,
        in_specs=placed,
        out_specs=(P("gran", "band", None, None), P("gran", "band", None, None)),
        check_vma=False,
    )
```

```python
import jax
import jax.numpy as jnp
from jax import lax
from jax.experimental import pallas as pl
from jax.experimental.pallas import tpu as pltpu
from jax.sharding import PartitionSpec as P

MESH = pl.DeviceIdType.MESH
F32 = jnp.float32
BF16 = jnp.bfloat16
I32 = jnp.int32

BANDS = 12
PATCH = 8
REACH = 4
SWEEPS = 3
SP = 32
ROBUST = 0.3 * BANDS * PATCH * PATCH

GD = 16
BD_ = 3
NG = 32
NB = 4
SLOTS = 8
PIX = 256
WIN = 16
FIRST_MAX = 64 - WIN
FAR = 1000.0
FAR_STEPS = 4
TILE_VMEM = 14 * 1024 * 1024


def iota(shape, dim):
    return lax.broadcasted_iota(I32, shape, dim)


def dot(a, b):
    return jnp.dot(a, b, preferred_element_type=F32)


def butterfly(x, lane, width, op):
    size = x.shape[1]
    step = 1
    while step < width:
        other = jnp.where(
            (lane // step) % 2 == 0,
            pltpu.roll(x, size - step, axis=1),
            pltpu.roll(x, step, axis=1),
        )
        x = op(x, other)
        step *= 2
    return x


def far_tap(d):
    return ((-0.5 * d + 2.5) * d - 4.0) * d + 2.0


def near_tap(d):
    return (1.5 * d - 2.5) * d * d + 1.0


PARTS = ((4, 8), (0, 4), (12, 4))


def packing(part):
    count = PARTS[part][1]
    blocks = 16 // count
    return count, blocks, 64 // blocks


def kernel(
    off_h,
    cnt_h,
    prior_h,
    rhs_h,
    diag_h,
    cross_h,
    coup_h,
    route_h,
    win_h,
    bal_h,
    pay_in,
    roww_h,
    colw_h,
    cover_h,
    off_s,
    cnt_s,
    route_v,
    win_v,
    prior_b,
    rhs_b,
    diag_b,
    cross_b,
    coup_b,
    out_b,
    grids,
    resp,
    coup,
    cterm,
    disp,
    spread,
    weight,
    halo_out,
    halo_in,
    part_out,
    part_in,
    tab_v,
    tab_s,
    pay_out,
    roww,
    colw,
    colt,
    cover_v,
    in_sem,
    out_sem,
    hs_sem,
    hr_sem,
    ps_sem,
    pr_sem,
    as_sem,
    ar_sem,
    tab_sem,
    own_sem,
    far_sem,
):
    me = lax.axis_index("gran")
    mb = lax.axis_index("band")
    right = lax.rem(me + 1, NG)
    left = lax.rem(me + NG - 1, NG)

    barrier = pltpu.get_barrier_semaphore()
    for other in (left, right):
        pl.semaphore_signal(barrier, inc=1, device_id=(other, mb), device_id_type=MESH)
    for k in range(1, NB):
        pl.semaphore_signal(
            barrier, inc=1, device_id=(me, lax.rem(mb + k, NB)), device_id_type=MESH
        )

    def far_signal(step):
        distance = 1 << step
        for side, shift in enumerate((distance, NG - distance)):
            pl.semaphore_signal(
                far_sem.at[step, side],
                inc=1,
                device_id=(lax.rem(me + shift, NG), mb),
                device_id_type=MESH,
            )

    def far_wait(step):
        for side in range(2):
            pl.semaphore_wait(far_sem.at[step, side], 1)

    ends = (pl.ds(0, REACH), pl.ds(GD - REACH, REACH))
    middle = pl.ds(REACH, GD - 2 * REACH)
    pairs = [(prior_h.at[part], prior_b.at[part]) for part in (*ends, middle)]
    pairs += [
        (off_h, off_s),
        (cnt_h, cnt_s),
        (coup_h, coup_b),
        (diag_h, diag_b),
        (cross_h, cross_b),
        (rhs_h, rhs_b),
        (route_h, route_v),
        (win_h, win_v),
    ]
    loads = [
        pltpu.make_async_copy(src, dst, in_sem.at[n]) for n, (src, dst) in enumerate(pairs)
    ]
    for load in loads[:2]:
        load.start()

    lane128 = iota((128, 128), 1)
    sub128 = iota((128, 128), 0)
    gather_table = ((sub128 % 64) // 8 == lane128 % 8).astype(F32).astype(BF16)
    spread_table = ((lane128 % 64) // 8 == sub128 % 8).astype(F32).astype(BF16)

    def take_prior(i):
        for b in range(BD_):
            for v in range(4):
                g0 = prior_b[i, b, pl.ds(2 * v, 8, stride=8), :]
                g1 = prior_b[i, b, pl.ds(2 * v + 1, 8, stride=8), :]
                grids[0, REACH + i, b, 0, v] = g0
                grids[0, REACH + i, b, 1, v] = g1
                resp[REACH + i, b, v] = g0 + g1

    def halo_rows(sweep, side, e, i):
        for b in range(BD_):
            halo_out[sweep, side, 0, e, b] = resp[REACH + i, b].reshape(32, 128).astype(BF16)
            halo_out[sweep, side, 1, e, b] = (
                grids[sweep % 2, REACH + i, b, 0].reshape(32, 128).astype(BF16)
            )

    for load in loads[:2]:
        load.wait()
    for load in loads[2:]:
        load.start()
    for side, base in ((1, 0), (0, GD - REACH)):

        def first_halo(e, carry, side=side, base=base):
            take_prior(base + e)
            halo_rows(0, side, e, base + e)
            return carry

        lax.fori_loop(0, REACH, first_halo, 0)

    pl.semaphore_wait(barrier, 2 + NB - 1)

    def halo_copy(sweep, side, piece):
        whole = not isinstance(piece, jax.Array) and piece == REACH
        part = (sweep, side, 1) if whole else (sweep, side, 0, piece)
        return pltpu.make_async_remote_copy(
            src_ref=halo_out.at[part],
            dst_ref=halo_in.at[part],
            send_sem=hs_sem.at[sweep, side, piece],
            recv_sem=hr_sem.at[sweep, side, piece],
            device_id=(right if side == 0 else left, mb),
            device_id_type=MESH,
        )

    def part_copy(sweep, part, k):
        return pltpu.make_async_remote_copy(
            src_ref=part_out.at[sweep, part, pl.ds(0, packing(part)[2])],
            dst_ref=part_in.at[sweep, part, k - 1, pl.ds(0, packing(part)[2])],
            send_sem=ps_sem.at[sweep, part, k - 1],
            recv_sem=pr_sem.at[sweep, part, k - 1],
            device_id=(me, lax.rem(mb + k, NB)),
            device_id_type=MESH,
        )

    for piece in range(REACH + 1):
        for side in range(2):
            halo_copy(0, side, piece).start()
    far_signal(0)

    for load in loads[2:5]:
        load.wait()

    def rest(k, carry):
        take_prior(REACH + k)
        return carry

    lax.fori_loop(0, GD - 2 * REACH, rest, 0)

    for part in range(3):
        count, blocks, rows = packing(part)
        lane_block = iota((rows, 128), 1) // 8
        slot = (lane_block // count) * (SLOTS // blocks) + iota((rows, 128), 0) // 8
        counts = jnp.zeros((rows, 128), I32)
        for k in range(count):
            counts = jnp.where(lane_block % count == k, cnt_s[PARTS[part][0] + k], counts)
        weight[part, :rows] = (slot < counts).astype(F32)

    def disparity(part, sweep):
        base = PARTS[part][0]
        count, blocks, height = packing(part)

        def one(k, carry):
            i = base + k
            own = [resp[REACH + i, b] for b in range(BD_)]
            for s in range(SLOTS):
                n = REACH + i + off_s[s, i]
                total = None
                for b in range(BD_):
                    diff = own[b] - resp[n, b]
                    square = diff * diff
                    total = square if total is None else total + square
                disp[pl.ds(pl.multiple_of(k * 64 + s * 8, 8), 8), :] = (
                    total[0] + total[1] + total[2] + total[3]
                )
            return carry

        lax.fori_loop(0, count, one, 0)
        sums = dot(disp[: count * 64].astype(BF16), gather_table)
        packed = jnp.zeros((height, 128), F32)
        lane_block = iota((height, 128), 1) // 8
        for k in range(count):
            for h in range(blocks):
                at = k * 64 + h * height
                packed = jnp.where(lane_block == h * count + k, sums[at : at + height], packed)
        part_out[sweep, part, :height] = packed.astype(BF16)
        for k in (2, 1, 3):
            part_copy(sweep, part, k).start()

    def solve(part, sweep):
        base = PARTS[part][0]
        count, blocks, height = packing(part)
        now, later = sweep % 2, (sweep + 1) % 2
        last = sweep == SWEEPS - 1
        for k in range(1, NB):
            part_copy(sweep, part, k).wait_recv()
        total = part_out[sweep, part, :height].astype(F32)
        for k in range(NB - 1):
            total = total + part_in[sweep, part, k, :height].astype(F32)
        robust = weight[part, :height] / (1.0 + total * (1.0 / ROBUST))
        lane_block = iota((height, 128), 1) // 8
        rows = []
        for k in range(count):
            for h in range(blocks):
                rows.append(jnp.where(lane_block == h * count + k, robust, 0.0))
        spread[: count * 64] = dot(jnp.concatenate(rows, axis=0).astype(BF16), spread_table)

        def one(k, carry):
            i = base + k
            places = [REACH + i + off_s[s, i] for s in range(SLOTS)]
            for b in range(BD_):
                sigma = drive0 = drive1 = None
                for s in range(SLOTS):
                    rob = spread[pl.ds(pl.multiple_of(k * 64 + s * 8, 8), 8), :]
                    eff = rob[None] * coup[i, b, s]
                    add0 = eff * grids[now, places[s], b, 0]
                    add1 = eff * grids[now, places[s], b, 1]
                    if s == 0:
                        sigma, drive0, drive1 = eff, add0, add1
                    else:
                        sigma, drive0, drive1 = sigma + eff, drive0 + add0, drive1 + add1
                for v in range(4):
                    even = pl.ds(2 * v, 8, stride=8)
                    odd = pl.ds(2 * v + 1, 8, stride=8)
                    r0 = rhs_b[i, b, even, :] + drive0[v]
                    r1 = rhs_b[i, b, odd, :] + drive1[v]
                    first = diag_b[i, b, even, :] + sigma[v]
                    second = diag_b[i, b, odd, :] + sigma[v]
                    cross = cterm[i, b, v]
                    inverse = 1.0 / (first * second - cross * cross)
                    g0 = (second * r0 - cross * r1) * inverse
                    g1 = (first * r1 - cross * r0) * inverse
                    if last:
                        out_b[i, b, even, :] = g0
                        out_b[i, b, odd, :] = g1
                    else:
                        grids[later, REACH + i, b, 0, v] = g0
                        grids[later, REACH + i, b, 1, v] = g1
                        resp[REACH + i, b, v] = g0 + g1
            if part > 0 and not last:
                halo_rows(sweep + 1, 2 - part, k, i)
                halo_copy(sweep + 1, 2 - part, k).start()
            return carry

        lax.fori_loop(0, count, one, 0)
        if part > 0 and not last:
            halo_copy(sweep + 1, 2 - part, REACH).start()

    def take_responses(sweep, side):
        def one(e, carry):
            halo_copy(sweep, side, e).wait_recv()
            for b in range(BD_):
                value = halo_in[sweep, side, 0, e, b].astype(F32)
                resp[e + side * (REACH + GD), b] = value.reshape(4, 8, 128)
            return carry

        lax.fori_loop(0, REACH, one, 0)

    def take_grids(sweep, side):
        now = sweep % 2
        halo_copy(sweep, side, REACH).wait_recv()

        def one(e, carry):
            place = e + side * (REACH + GD)
            for b in range(BD_):
                g0 = halo_in[sweep, side, 1, e, b].astype(F32).reshape(4, 8, 128)
                grids[now, place, b, 0] = g0
                grids[now, place, b, 1] = resp[place, b] - g0
            return carry

        lax.fori_loop(0, REACH, one, 0)

    def take_coupling():
        row = iota((256, 256), 0)
        source = (4 * (row % 8) + (row // 8) % 4) * 8 + row // 32
        order = (iota((256, 256), 1) == source).astype(F32).astype(BF16)

        def one(i, carry):
            for b in range(BD_):
                both = jnp.concatenate([coup_b[i, b], coup_b[i + 8, b]], axis=1)
                moved = dot(order, both)
                coup[i, b] = moved[:, :128].reshape(SLOTS, 4, 8, 128)
                coup[i + 8, b] = moved[:, 128:].reshape(SLOTS, 4, 8, 128)
            return carry

        lax.fori_loop(0, GD // 2, one, 0)

    def take_cross():
        def one(half, carry):
            for g in range(8):
                i = half * 8 + g
                for b in range(BD_):
                    for v in range(4):
                        d0 = diag_b[i, b, pl.ds(2 * v, 8, stride=8), :]
                        d1 = diag_b[i, b, pl.ds(2 * v + 1, 8, stride=8), :]
                        value = cross_b[b, half, pl.ds(8 * v + g, 8, stride=32), :]
                        cterm[i, b, v] = value * jnp.sqrt(d0 * d1)
            return carry

        lax.fori_loop(0, 2, one, 0)

    def send_table():
        block = pl.multiple_of((me // 8) * 128, 128)
        turn = lax.rem(128 - lax.rem(me, 8) * 16, 128)
        lane = iota((32, 128), 1)
        tile = iota((32, 128), 0)

        def own(ref_rows):
            pair = []
            for route in range(2):
                row = jnp.broadcast_to(ref_rows(route, pl.ds(block, 128)), (32, 128))
                row = pltpu.roll(row, turn, axis=1)
                pair.append(pltpu.roll(row, 16, axis=1) if route else row)
            return jnp.where(lane < 16, pair[0], pair[1])

        routes = own(lambda route, cols: route_v[pl.ds(route, 1), cols])
        starts = [
            own(lambda route, cols, c=c: win_v[route, pl.ds(c, 1), cols]) for c in range(2)
        ]
        match = (routes == tile) & (lane < 32)
        low = butterfly(jnp.where(match, lane, 99), lane, 32, jnp.minimum)
        high = butterfly(jnp.where(match, lane, -1), lane, 32, jnp.maximum)
        table = jnp.zeros((32, 128), I32)
        for rank, chosen in enumerate((low, high)):
            picks = [
                butterfly(
                    jnp.where((lane == chosen) & (lane < 32), start, 0), lane, 32, jnp.add
                )
                for start in starts
            ]
            valid = (chosen >= 0) & (chosen < 32)
            granule = jnp.where(valid, chosen % 16, 0)
            first = [jnp.clip(pick // SP - 1, 0, FIRST_MAX) for pick in picks]
            turns = [(b * 16 + 128 - first[1]) % 128 for b in range(BD_)]
            for column, value in enumerate((granule, (first[0] // 2) * 2, *turns)):
                table = jnp.where(lane == rank * 5 + column, value, table)
        tab_v[...] = table
        copy = pltpu.make_async_copy(tab_v, tab_s, tab_sem)
        copy.start()
        copy.wait()

    def weights(coord, ref):
        lane = iota((8, 512), 1)
        place = lane % 16
        match = []
        for route in range(2):
            row = jnp.broadcast_to(route_v[pl.ds(route, 1), :], (8, 512))
            match.append(row == me)
        low = jnp.minimum(
            jnp.where(match[0], place, 99), jnp.where(match[1], place + 16, 99)
        )
        high = jnp.maximum(
            jnp.where(match[0], place, -1), jnp.where(match[1], place + 16, -1)
        )
        low = butterfly(low, lane, 16, jnp.minimum)
        high = butterfly(high, lane, 16, jnp.maximum)
        total = jnp.sum(
            (match[0].astype(F32) + match[1].astype(F32))[0:1], axis=1, keepdims=True
        )
        for rank, chosen in enumerate((low, high)):
            live = (chosen < 32) if rank == 0 else (high != low) & (chosen >= 0)
            if True:
                pick = jnp.zeros((8, 512), I32)
                for route in range(2):
                    row = jnp.broadcast_to(win_v[route, pl.ds(coord, 1), :], (8, 512))
                    pick = pick + jnp.where(chosen == place + 16 * route, row, 0)
                pick = butterfly(pick, lane, 16, jnp.add)
                first = jnp.clip(pick // SP - 1, 0, FIRST_MAX)
                if coord == 0:
                    knot = (first // 2) * 2 + 2 * (place % 8) + place // 8
                else:
                    knot = first + place
                knot_f = knot.astype(F32)
                extra = jnp.where(
                    knot == 0, -1.0, jnp.where(knot == 63, 64.0, FAR)
                )
                start = pick.astype(F32) * (1.0 / SP)
                lead = start - knot_f
                lead_extra = start - extra

                def rows(block, carry, ref=ref, rank=rank, lead=lead, lead_extra=lead_extra,
                         live=live, coord=coord):
                    parts = []
                    for h in range(2):
                        pixel = (
                            iota((8, 512), 0) + (block * 16 + h * 8)
                        ).astype(F32) * (1.0 / SP)
                        d = jnp.abs(lead + pixel)
                        w = jnp.where(d <= 1.0, near_tap(d), far_tap(d))
                        w = jnp.where(d < 2.0, w, 0.0)
                        d2 = jnp.abs(lead_extra + pixel)
                        w = w + jnp.where(d2 < 2.0, far_tap(d2), 0.0)
                        if coord == 1:
                            w = jnp.where(live, w, 0.0)
                        parts.append(w)
                    ref[pl.ds(pl.multiple_of(block * 16, 16), 16), rank * 512 : rank * 512 + 512] = (
                        jnp.concatenate(parts, axis=0).astype(BF16)
                    )
                    return carry

                lax.fori_loop(0, PIX // 16, rows, 0)
        cover_v[...] = jnp.broadcast_to(1.0 / total, (8, 128))

    saves = [
        pltpu.make_async_copy(src, dst, out_sem.at[n])
        for n, (src, dst) in enumerate(
            ((roww, roww_h), (colt, colw_h), (cover_v, cover_h), (out_b, bal_h))
        )
    ]
    for sweep in range(SWEEPS):
        order = (1, 2) if sweep % 2 == 0 else (2, 1)
        disparity(0, sweep)
        if sweep == 0:
            loads[5].wait()
            take_coupling()
        elif sweep == 1:
            far_wait(1)
            far_signal(2)
            loads[9].wait()
            loads[10].wait()
            weights(0, roww)
            saves[0].start()
        else:
            weights(1, colw)
            colt[...] = colw[...].T
            saves[1].start()
            saves[2].start()
        for step, part in enumerate(order):
            take_responses(sweep, part - 1)
            if step == 0 and sweep < 2:
                far_wait(2 * sweep)
                far_signal(2 * sweep + 1)
            disparity(part, sweep)
        if sweep == 0:
            loads[6].wait()
            loads[7].wait()
            take_cross()
            loads[8].wait()
        solve(0, sweep)
        if sweep == 2:
            send_table()
            far_wait(3)
        for part in order:
            take_grids(sweep, part - 1)
            solve(part, sweep)
    saves[3].start()

    lane8 = iota((8, 128), 1)
    lane_band = (lane8 % 64) // 16

    def fill(t):
        for rank in range(2):
            granule = tab_s[t, rank * 5]
            row = tab_s[t, rank * 5 + 1]
            halves = []
            for c in range(2):
                value = None
                for b in range(BD_):
                    x = out_b[granule, b, pl.ds(row + c, 8, stride=2), :]
                    x = pltpu.roll(x, tab_s[t, rank * 5 + 2 + b], axis=1)
                    value = x if value is None else jnp.where(lane_band == b, x, value)
                halves.append(value)
            pay_out[t, rank * 16 : rank * 16 + 16, :] = jnp.concatenate(halves, axis=0).astype(BF16)

    def pay_copy(k):
        return pltpu.make_async_remote_copy(
            src_ref=pay_out.at[lax.rem(me + k, NG)],
            dst_ref=pay_in.at[me],
            send_sem=as_sem.at[k],
            recv_sem=ar_sem.at[k],
            device_id=(lax.rem(me + k, NG), mb),
            device_id_type=MESH,
        )

    def fill_and_send(n, carry):
        steps = [lax.rem(12 + n * 4 + u, NG) for u in range(4)]
        for k in steps:
            fill(lax.rem(me + k, NG))
        for k in steps:

            @pl.when(k > 0)
            def _(k=k):
                pay_copy(k).start()

        return carry

    lax.fori_loop(0, NG // 4, fill_and_send, 0)
    own_copy = pltpu.make_async_copy(pay_out.at[me], pay_in.at[me], own_sem)
    own_copy.start()
    own_copy.wait()
    for sweep in range(SWEEPS):
        for side in range(2):
            for piece in range(REACH + 1):
                halo_copy(sweep, side, piece).wait_send()
        for part in range(3):
            for k in range(1, NB):
                part_copy(sweep, part, k).wait_send()
    for save in saves:
        save.wait()

    def take_pay(k, carry):
        pltpu.make_async_remote_copy(
            src_ref=pay_out.at[lax.rem(me + k, NG)],
            dst_ref=pay_in.at[lax.rem(me + NG - k, NG)],
            send_sem=as_sem.at[k],
            recv_sem=ar_sem.at[k],
            device_id=(lax.rem(me + k, NG), mb),
            device_id_type=MESH,
        ).wait_recv()
        return carry

    lax.fori_loop(1, NG, take_pay, 0)

    def sent_pay(k, carry):
        pay_copy(k).wait_send()
        return carry

    lax.fori_loop(1, NG, sent_pay, 0)


def tile_kernel(
    pay_h,
    roww_h,
    colw_h,
    cover_h,
    pix_h,
    mid_h,
    bal_h,
    tile_h,
    pay_in,
    roww,
    colw,
    cover,
    pix_b,
    bal_b,
    tile_b,
    diagonal,
    rowpass,
    in_sem,
    out_sem,
):
    quarter = [pl.ds(4 * n, 4) for n in range(4)]
    pairs = [
        (pay_h, pay_in),
        (roww_h, roww),
        (colw_h, colw),
        (cover_h, cover),
        (pix_h, pix_b),
    ] + [(mid_h.at[part], bal_b.at[part]) for part in quarter]
    loads = [
        pltpu.make_async_copy(src, dst, in_sem.at[n]) for n, (src, dst) in enumerate(pairs)
    ]
    for load in loads:
        load.start()
    saves = [
        pltpu.make_async_copy(bal_b.at[part], bal_h.at[part], out_sem.at[n])
        for n, part in enumerate(quarter)
    ]

    def clear(n, carry):
        diagonal[n] = jnp.zeros((256, 256), BF16)
        return carry

    lax.fori_loop(0, 24, clear, 0)
    lane8 = iota((8, 128), 1)
    loads[0].wait()

    def expand(b):
        for group in range(4):
            rank, base = group // 2, (group % 2) * 16
            for s in range(16):
                block = pay_in[base + s, rank * 16 : rank * 16 + 16, :].astype(F32)
                for c in range(2):
                    parts = []
                    for parity in range(2):
                        turn = ((s % 8) * 16 - parity * 64 - b * 16) % 128
                        y = block[c * 8 : c * 8 + 8]
                        y = pltpu.roll(y, turn, axis=1) if turn else y
                        parts.append(jnp.where(lane8 // 16 == s % 8, y, 0.0))
                    diagonal[
                        group * 6 + b * 2 + c,
                        s * 16 : s * 16 + 16,
                        (s // 8) * 128 : (s // 8) * 128 + 128,
                    ] = jnp.concatenate(parts, axis=0).astype(BF16)

    expand(0)
    for load in loads[1:4]:
        load.wait()
    for load, save in zip(loads[5:], saves):
        load.wait()
        save.start()
    loads[4].wait()
    inverse_cover = cover[0:1, 0:1]

    for b in range(BD_):
        if b + 1 < BD_:
            expand(b + 1)
        fields = []
        for c in range(2):
            for group in range(4):
                cols = slice(group * 256, group * 256 + 256)
                rowpass[:, cols] = dot(roww[:, cols], diagonal[group * 6 + b * 2 + c]).astype(BF16)
            fields.append(dot(rowpass[...], colw[...]))
        pixels = pix_b[b].astype(F32)
        value = pixels * (1.0 + fields[0] * inverse_cover) + fields[1] * inverse_cover
        tile_b[b] = value.astype(BF16)
        pltpu.make_async_copy(tile_b.at[b], tile_h.at[b], out_sem.at[4 + b]).start()

    for save in saves:
        save.wait()
    for b in range(BD_):
        pltpu.make_async_copy(tile_b.at[b], tile_h.at[b], out_sem.at[4 + b]).wait()


def per_device(
    prior_grids,
    pif_rhs,
    pif_diagonal,
    pif_cross,
    pif_coupling,
    neighbour_offset,
    neighbour_count,
    tile_route,
    tile_window,
    tile_pixels,
):
    def pairs(x):
        return x.reshape(GD, BD_, 2, 32, 128).transpose(0, 1, 3, 2, 4).reshape(GD, BD_, 64, 128)

    prior = pairs(prior_grids)
    rhs = pairs(pif_rhs)
    diag = pairs(pif_diagonal)
    cross = (
        pif_cross.reshape(2, 8, BD_, 32, 128).transpose(2, 0, 3, 1, 4).reshape(BD_, 2, 256, 128)
    )
    coupling = (
        pif_coupling.reshape(GD, SLOTS, BD_, 32, 128)
        .transpose(0, 2, 3, 1, 4)
        .reshape(GD, BD_, 256, 128)
    )
    any_ = pl.BlockSpec(memory_space=pl.ANY)
    hbm = pl.BlockSpec(memory_space=pltpu.HBM)
    dma = pltpu.SemaphoreType.DMA
    middle, payload, roww, colw, cover = pl.pallas_call(
        kernel,
        out_shape=(
            jax.ShapeDtypeStruct((GD, BD_, 64, 128), F32),
            jax.ShapeDtypeStruct((NG, 32, 128), BF16),
            jax.ShapeDtypeStruct((PIX, 1024), BF16),
            jax.ShapeDtypeStruct((1024, PIX), BF16),
            jax.ShapeDtypeStruct((8, 128), F32),
        ),
        in_specs=[hbm] * 9,
        out_specs=(any_,) * 5,
        scratch_shapes=[
            pltpu.SMEM((SLOTS, GD), I32),
            pltpu.SMEM((GD,), I32),
            pltpu.VMEM((2, NG * GD), I32),
            pltpu.VMEM((2, 2, NG * GD), I32),
            pltpu.VMEM((GD, BD_, 64, 128), F32),
            pltpu.VMEM((GD, BD_, 64, 128), F32),
            pltpu.VMEM((GD, BD_, 64, 128), F32),
            pltpu.VMEM((BD_, 2, 256, 128), F32),
            pltpu.VMEM((GD, BD_, 256, 128), BF16),
            pltpu.VMEM((GD, BD_, 64, 128), F32),
            pltpu.VMEM((2, GD + 2 * REACH, BD_, 2, 4, 8, 128), F32),
            pltpu.VMEM((GD + 2 * REACH, BD_, 4, 8, 128), F32),
            pltpu.VMEM((GD, BD_, SLOTS, 4, 8, 128), F32),
            pltpu.VMEM((GD, BD_, 4, 8, 128), F32),
            pltpu.VMEM((512, 128), F32),
            pltpu.VMEM((512, 128), F32),
            pltpu.VMEM((3, 32, 128), F32),
            pltpu.VMEM((SWEEPS, 2, 2, REACH, BD_, 32, 128), BF16),
            pltpu.VMEM((SWEEPS, 2, 2, REACH, BD_, 32, 128), BF16),
            pltpu.VMEM((SWEEPS, 3, 32, 128), BF16),
            pltpu.VMEM((SWEEPS, 3, NB - 1, 32, 128), BF16),
            pltpu.VMEM((NG, 128), I32),
            pltpu.SMEM((NG, 128), I32),
            pltpu.VMEM((NG, 32, 128), BF16),
            pltpu.VMEM((PIX, 1024), BF16),
            pltpu.VMEM((PIX, 1024), BF16),
            pltpu.VMEM((1024, PIX), BF16),
            pltpu.VMEM((8, 128), F32),
            dma((11,)),
            dma((4,)),
            dma((SWEEPS, 2, REACH + 1)),
            dma((SWEEPS, 2, REACH + 1)),
            dma((SWEEPS, 3, NB - 1)),
            dma((SWEEPS, 3, NB - 1)),
            dma((NG,)),
            dma((NG,)),
            dma,
            dma,
            pltpu.SemaphoreType.REGULAR((FAR_STEPS, 2)),
        ],
        compiler_params=pltpu.CompilerParams(
            collective_id=0, has_side_effects=True, vmem_limit_bytes=36 * 1024 * 1024
        ),
        name="balance",
    )(
        *(
            pltpu.with_memory_space_constraint(x, pltpu.HBM)
            for x in (
                neighbour_offset.T,
                neighbour_count,
                prior,
                rhs,
                diag,
                cross,
                coupling,
                tile_route.T,
                tile_window.transpose(1, 2, 0),
            )
        )
    )
    balanced, tiles = pl.pallas_call(
        tile_kernel,
        out_shape=(
            jax.ShapeDtypeStruct((GD, BD_, 64, 128), F32),
            jax.ShapeDtypeStruct((BD_, PIX, PIX), BF16),
        ),
        in_specs=[any_] * 6,
        out_specs=(any_, any_),
        scratch_shapes=[
            pltpu.VMEM((NG, 32, 128), BF16),
            pltpu.VMEM((PIX, 1024), BF16),
            pltpu.VMEM((1024, PIX), BF16),
            pltpu.VMEM((8, 128), F32),
            pltpu.VMEM((BD_, PIX, PIX), BF16),
            pltpu.VMEM((GD, BD_, 64, 128), F32),
            pltpu.VMEM((BD_, PIX, PIX), BF16),
            pltpu.VMEM((24, 256, 256), BF16),
            pltpu.VMEM((PIX, 1024), BF16),
            dma((9,)),
            dma((7,)),
        ],
        compiler_params=pltpu.CompilerParams(vmem_limit_bytes=TILE_VMEM),
        name="tiles",
    )(payload, roww, colw, cover, tile_pixels[0], middle)
    balanced = (
        balanced.reshape(GD, BD_, 32, 2, 128)
        .transpose(0, 1, 3, 2, 4)
        .reshape(GD, BD_, 2, 4096)
    )
    return (balanced, tiles[None])


def solution(mesh):
    placed = (
        P("gran", "band", None, None),
        P("gran", "band", None, None),
        P("gran", "band", None, None),
        P("gran", "band", None),
        P("gran", None, "band", None),
        P("gran", None),
        P("gran"),
        P(),
        P(),
        P("gran", "band", None, None),
    )
    return jax.shard_map(
        per_device,
        mesh=mesh,
        in_specs=placed,
        out_specs=(P("gran", "band", None, None), P("gran", "band", None, None)),
        check_vma=False,
    )
```

```python
import jax
import jax.numpy as jnp
from jax import lax
from jax.experimental import pallas as pl
from jax.experimental.pallas import tpu as pltpu
from jax.sharding import PartitionSpec as P

MESH = pl.DeviceIdType.MESH
F32 = jnp.float32
BF16 = jnp.bfloat16
I32 = jnp.int32

BANDS = 12
PATCH = 8
REACH = 4
SWEEPS = 3
SP = 32
ROBUST = 0.3 * BANDS * PATCH * PATCH

GD = 16
BD_ = 3
NG = 32
NB = 4
SLOTS = 8
PIX = 256
WIN = 16
FIRST_MAX = 64 - WIN
FAR = 1000.0
FAR_STEPS = 4
TILE_VMEM = 14 * 1024 * 1024


def iota(shape, dim):
    return lax.broadcasted_iota(I32, shape, dim)


def dot(a, b):
    return jnp.dot(a, b, preferred_element_type=F32)


def butterfly(x, lane, width, op):
    size = x.shape[1]
    step = 1
    while step < width:
        other = jnp.where(
            (lane // step) % 2 == 0,
            pltpu.roll(x, size - step, axis=1),
            pltpu.roll(x, step, axis=1),
        )
        x = op(x, other)
        step *= 2
    return x


def far_tap(d):
    return ((-0.5 * d + 2.5) * d - 4.0) * d + 2.0


def near_tap(d):
    return (1.5 * d - 2.5) * d * d + 1.0


PARTS = ((4, 8), (0, 4), (12, 4))


def packing(part):
    count = PARTS[part][1]
    blocks = 16 // count
    return count, blocks, 64 // blocks


def kernel(
    off_h,
    cnt_h,
    prior_h,
    rhs_h,
    diag_h,
    cross_h,
    coup_h,
    route_h,
    win_h,
    bal_h,
    pay_in,
    roww_h,
    colw_h,
    cover_h,
    off_s,
    cnt_s,
    route_v,
    win_v,
    prior_b,
    rhs_b,
    diag_b,
    cross_b,
    coup_b,
    out_b,
    grids,
    resp,
    coup,
    cterm,
    disp,
    spread,
    weight,
    halo_out,
    halo_in,
    part_out,
    part_in,
    tab_v,
    tab_s,
    pay_out,
    roww,
    colw,
    colt,
    cover_v,
    in_sem,
    out_sem,
    hs_sem,
    hr_sem,
    ps_sem,
    pr_sem,
    as_sem,
    ar_sem,
    tab_sem,
    own_sem,
    far_sem,
):
    me = lax.axis_index("gran")
    mb = lax.axis_index("band")
    right = lax.rem(me + 1, NG)
    left = lax.rem(me + NG - 1, NG)

    barrier = pltpu.get_barrier_semaphore()
    for other in (left, right):
        pl.semaphore_signal(barrier, inc=1, device_id=(other, mb), device_id_type=MESH)
    for k in range(1, NB):
        pl.semaphore_signal(
            barrier, inc=1, device_id=(me, lax.rem(mb + k, NB)), device_id_type=MESH
        )

    def far_signal(step):
        distance = 1 << step
        for side, shift in enumerate((distance, NG - distance)):
            pl.semaphore_signal(
                far_sem.at[step, side],
                inc=1,
                device_id=(lax.rem(me + shift, NG), mb),
                device_id_type=MESH,
            )

    def far_wait(step):
        for side in range(2):
            pl.semaphore_wait(far_sem.at[step, side], 1)

    ends = (pl.ds(0, REACH), pl.ds(GD - REACH, REACH))
    middle = pl.ds(REACH, GD - 2 * REACH)
    pairs = [(prior_h.at[part], prior_b.at[part]) for part in (*ends, middle)]
    pairs += [
        (off_h, off_s),
        (cnt_h, cnt_s),
        (coup_h, coup_b),
        (diag_h, diag_b),
        (cross_h, cross_b),
        (rhs_h, rhs_b),
        (route_h, route_v),
        (win_h, win_v),
    ]
    loads = [
        pltpu.make_async_copy(src, dst, in_sem.at[n]) for n, (src, dst) in enumerate(pairs)
    ]
    for load in loads[:2]:
        load.start()

    lane128 = iota((128, 128), 1)
    sub128 = iota((128, 128), 0)
    gather_table = ((sub128 % 64) // 8 == lane128 % 8).astype(F32).astype(BF16)
    spread_table = ((lane128 % 64) // 8 == sub128 % 8).astype(F32).astype(BF16)

    def take_prior(i):
        for b in range(BD_):
            for v in range(4):
                g0 = prior_b[i, b, pl.ds(2 * v, 8, stride=8), :]
                g1 = prior_b[i, b, pl.ds(2 * v + 1, 8, stride=8), :]
                grids[0, REACH + i, b, 0, v] = g0
                grids[0, REACH + i, b, 1, v] = g1
                resp[REACH + i, b, v] = g0 + g1

    def halo_rows(sweep, side, e, i):
        for b in range(BD_):
            halo_out[sweep, side, 0, e, b] = resp[REACH + i, b].reshape(32, 128).astype(BF16)
            halo_out[sweep, side, 1, e, b] = (
                grids[sweep % 2, REACH + i, b, 0].reshape(32, 128).astype(BF16)
            )

    for load in loads[:2]:
        load.wait()
    for load in loads[2:]:
        load.start()
    for side, base in ((1, 0), (0, GD - REACH)):

        def first_halo(e, carry, side=side, base=base):
            take_prior(base + e)
            halo_rows(0, side, e, base + e)
            return carry

        lax.fori_loop(0, REACH, first_halo, 0)

    pl.semaphore_wait(barrier, 2 + NB - 1)

    def halo_copy(sweep, side, piece):
        whole = not isinstance(piece, jax.Array) and piece == REACH
        part = (sweep, side, 1) if whole else (sweep, side, 0, piece)
        return pltpu.make_async_remote_copy(
            src_ref=halo_out.at[part],
            dst_ref=halo_in.at[part],
            send_sem=hs_sem.at[sweep, side, piece],
            recv_sem=hr_sem.at[sweep, side, piece],
            device_id=(right if side == 0 else left, mb),
            device_id_type=MESH,
        )

    def part_copy(sweep, part, k):
        return pltpu.make_async_remote_copy(
            src_ref=part_out.at[sweep, part, pl.ds(0, packing(part)[2])],
            dst_ref=part_in.at[sweep, part, k - 1, pl.ds(0, packing(part)[2])],
            send_sem=ps_sem.at[sweep, part, k - 1],
            recv_sem=pr_sem.at[sweep, part, k - 1],
            device_id=(me, lax.rem(mb + k, NB)),
            device_id_type=MESH,
        )

    for piece in range(REACH + 1):
        for side in range(2):
            halo_copy(0, side, piece).start()
    far_signal(0)

    for load in loads[2:5]:
        load.wait()

    def rest(k, carry):
        take_prior(REACH + k)
        return carry

    lax.fori_loop(0, GD - 2 * REACH, rest, 0)

    for part in range(3):
        count, blocks, rows = packing(part)
        lane_block = iota((rows, 128), 1) // 8
        slot = (lane_block // count) * (SLOTS // blocks) + iota((rows, 128), 0) // 8
        counts = jnp.zeros((rows, 128), I32)
        for k in range(count):
            counts = jnp.where(lane_block % count == k, cnt_s[PARTS[part][0] + k], counts)
        weight[part, :rows] = (slot < counts).astype(F32)

    def disparity(part, sweep):
        base = PARTS[part][0]
        count, blocks, height = packing(part)

        def one(k, carry):
            i = base + k
            own = [resp[REACH + i, b] for b in range(BD_)]
            for s in range(SLOTS):
                n = REACH + i + off_s[s, i]
                total = None
                for b in range(BD_):
                    diff = own[b] - resp[n, b]
                    square = diff * diff
                    total = square if total is None else total + square
                disp[pl.ds(pl.multiple_of(k * 64 + s * 8, 8), 8), :] = (
                    total[0] + total[1] + total[2] + total[3]
                )
            return carry

        lax.fori_loop(0, count, one, 0)
        sums = dot(disp[: count * 64].astype(BF16), gather_table)
        packed = jnp.zeros((height, 128), F32)
        lane_block = iota((height, 128), 1) // 8
        for k in range(count):
            for h in range(blocks):
                at = k * 64 + h * height
                packed = jnp.where(lane_block == h * count + k, sums[at : at + height], packed)
        part_out[sweep, part, :height] = packed.astype(BF16)
        for k in (2, 1, 3):
            part_copy(sweep, part, k).start()

    def solve(part, sweep):
        base = PARTS[part][0]
        count, blocks, height = packing(part)
        now, later = sweep % 2, (sweep + 1) % 2
        last = sweep == SWEEPS - 1
        for k in range(1, NB):
            part_copy(sweep, part, k).wait_recv()
        total = part_out[sweep, part, :height].astype(F32)
        for k in range(NB - 1):
            total = total + part_in[sweep, part, k, :height].astype(F32)
        robust = weight[part, :height] / (1.0 + total * (1.0 / ROBUST))
        lane_block = iota((height, 128), 1) // 8
        rows = []
        for k in range(count):
            for h in range(blocks):
                rows.append(jnp.where(lane_block == h * count + k, robust, 0.0))
        spread[: count * 64] = dot(jnp.concatenate(rows, axis=0).astype(BF16), spread_table)

        def one(k, carry):
            i = base + k
            places = [REACH + i + off_s[s, i] for s in range(SLOTS)]
            for b in range(BD_):
                sigma = drive0 = drive1 = None
                for s in range(SLOTS):
                    rob = spread[pl.ds(pl.multiple_of(k * 64 + s * 8, 8), 8), :]
                    eff = rob[None] * coup[i, b, s]
                    add0 = eff * grids[now, places[s], b, 0]
                    add1 = eff * grids[now, places[s], b, 1]
                    if s == 0:
                        sigma, drive0, drive1 = eff, add0, add1
                    else:
                        sigma, drive0, drive1 = sigma + eff, drive0 + add0, drive1 + add1
                for v in range(4):
                    even = pl.ds(2 * v, 8, stride=8)
                    odd = pl.ds(2 * v + 1, 8, stride=8)
                    r0 = rhs_b[i, b, even, :] + drive0[v]
                    r1 = rhs_b[i, b, odd, :] + drive1[v]
                    first = diag_b[i, b, even, :] + sigma[v]
                    second = diag_b[i, b, odd, :] + sigma[v]
                    cross = cterm[i, b, v]
                    inverse = 1.0 / (first * second - cross * cross)
                    g0 = (second * r0 - cross * r1) * inverse
                    g1 = (first * r1 - cross * r0) * inverse
                    if last:
                        out_b[i, b, even, :] = g0
                        out_b[i, b, odd, :] = g1
                    else:
                        grids[later, REACH + i, b, 0, v] = g0
                        grids[later, REACH + i, b, 1, v] = g1
                        resp[REACH + i, b, v] = g0 + g1
            if part > 0 and not last:
                halo_rows(sweep + 1, 2 - part, k, i)
                halo_copy(sweep + 1, 2 - part, k).start()
            return carry

        lax.fori_loop(0, count, one, 0)
        if part > 0 and not last:
            halo_copy(sweep + 1, 2 - part, REACH).start()

    def take_responses(sweep, side):
        def one(e, carry):
            halo_copy(sweep, side, e).wait_recv()
            for b in range(BD_):
                value = halo_in[sweep, side, 0, e, b].astype(F32)
                resp[e + side * (REACH + GD), b] = value.reshape(4, 8, 128)
            return carry

        lax.fori_loop(0, REACH, one, 0)

    def take_grids(sweep, side):
        now = sweep % 2
        halo_copy(sweep, side, REACH).wait_recv()

        def one(e, carry):
            place = e + side * (REACH + GD)
            for b in range(BD_):
                g0 = halo_in[sweep, side, 1, e, b].astype(F32).reshape(4, 8, 128)
                grids[now, place, b, 0] = g0
                grids[now, place, b, 1] = resp[place, b] - g0
            return carry

        lax.fori_loop(0, REACH, one, 0)

    def take_coupling():
        row = iota((256, 256), 0)
        source = (4 * (row % 8) + (row // 8) % 4) * 8 + row // 32
        order = (iota((256, 256), 1) == source).astype(F32).astype(BF16)

        def one(i, carry):
            for b in range(BD_):
                both = jnp.concatenate([coup_b[i, b], coup_b[i + 8, b]], axis=1)
                moved = dot(order, both)
                coup[i, b] = moved[:, :128].reshape(SLOTS, 4, 8, 128)
                coup[i + 8, b] = moved[:, 128:].reshape(SLOTS, 4, 8, 128)
            return carry

        lax.fori_loop(0, GD // 2, one, 0)

    def take_cross():
        def one(half, carry):
            for g in range(8):
                i = half * 8 + g
                for b in range(BD_):
                    for v in range(4):
                        d0 = diag_b[i, b, pl.ds(2 * v, 8, stride=8), :]
                        d1 = diag_b[i, b, pl.ds(2 * v + 1, 8, stride=8), :]
                        value = cross_b[b, half, pl.ds(8 * v + g, 8, stride=32), :]
                        cterm[i, b, v] = value * jnp.sqrt(d0 * d1)
            return carry

        lax.fori_loop(0, 2, one, 0)

    def send_table():
        block = pl.multiple_of((me // 8) * 128, 128)
        turn = lax.rem(128 - lax.rem(me, 8) * 16, 128)
        lane = iota((32, 128), 1)
        tile = iota((32, 128), 0)

        def own(ref_rows):
            pair = []
            for route in range(2):
                row = jnp.broadcast_to(ref_rows(route, pl.ds(block, 128)), (32, 128))
                row = pltpu.roll(row, turn, axis=1)
                pair.append(pltpu.roll(row, 16, axis=1) if route else row)
            return jnp.where(lane < 16, pair[0], pair[1])

        routes = own(lambda route, cols: route_v[pl.ds(route, 1), cols])
        starts = [
            own(lambda route, cols, c=c: win_v[route, pl.ds(c, 1), cols]) for c in range(2)
        ]
        match = (routes == tile) & (lane < 32)
        low = butterfly(jnp.where(match, lane, 99), lane, 32, jnp.minimum)
        high = butterfly(jnp.where(match, lane, -1), lane, 32, jnp.maximum)
        table = jnp.zeros((32, 128), I32)
        for rank, chosen in enumerate((low, high)):
            picks = [
                butterfly(
                    jnp.where((lane == chosen) & (lane < 32), start, 0), lane, 32, jnp.add
                )
                for start in starts
            ]
            valid = (chosen >= 0) & (chosen < 32)
            granule = jnp.where(valid, chosen % 16, 0)
            first = [jnp.clip(pick // SP - 1, 0, FIRST_MAX) for pick in picks]
            turns = [(b * 16 + 128 - first[1]) % 128 for b in range(BD_)]
            for column, value in enumerate((granule, (first[0] // 2) * 2, *turns)):
                table = jnp.where(lane == rank * 5 + column, value, table)
        tab_v[...] = table
        pltpu.make_async_copy(tab_v, tab_s, tab_sem).start()

    def weights(coord, ref):
        lane = iota((8, 512), 1)
        place = lane % 16
        match = []
        for route in range(2):
            row = jnp.broadcast_to(route_v[pl.ds(route, 1), :], (8, 512))
            match.append(row == me)
        low = jnp.minimum(
            jnp.where(match[0], place, 99), jnp.where(match[1], place + 16, 99)
        )
        high = jnp.maximum(
            jnp.where(match[0], place, -1), jnp.where(match[1], place + 16, -1)
        )
        low = butterfly(low, lane, 16, jnp.minimum)
        high = butterfly(high, lane, 16, jnp.maximum)
        total = jnp.sum(
            (match[0].astype(F32) + match[1].astype(F32))[0:1], axis=1, keepdims=True
        )
        for rank, chosen in enumerate((low, high)):
            live = (chosen < 32) if rank == 0 else (high != low) & (chosen >= 0)
            if True:
                pick = jnp.zeros((8, 512), I32)
                for route in range(2):
                    row = jnp.broadcast_to(win_v[route, pl.ds(coord, 1), :], (8, 512))
                    pick = pick + jnp.where(chosen == place + 16 * route, row, 0)
                pick = butterfly(pick, lane, 16, jnp.add)
                first = jnp.clip(pick // SP - 1, 0, FIRST_MAX)
                if coord == 0:
                    knot = (first // 2) * 2 + 2 * (place % 8) + place // 8
                else:
                    knot = first + place
                knot_f = knot.astype(F32)
                extra = jnp.where(
                    knot == 0, -1.0, jnp.where(knot == 63, 64.0, FAR)
                )
                start = pick.astype(F32) * (1.0 / SP)
                lead = start - knot_f
                lead_extra = start - extra

                def rows(block, carry, ref=ref, rank=rank, lead=lead, lead_extra=lead_extra,
                         live=live, coord=coord):
                    parts = []
                    for h in range(2):
                        pixel = (
                            iota((8, 512), 0) + (block * 16 + h * 8)
                        ).astype(F32) * (1.0 / SP)
                        d = jnp.abs(lead + pixel)
                        w = jnp.where(d <= 1.0, near_tap(d), far_tap(d))
                        w = jnp.where(d < 2.0, w, 0.0)
                        d2 = jnp.abs(lead_extra + pixel)
                        w = w + jnp.where(d2 < 2.0, far_tap(d2), 0.0)
                        if coord == 1:
                            w = jnp.where(live, w, 0.0)
                        parts.append(w)
                    ref[pl.ds(pl.multiple_of(block * 16, 16), 16), rank * 512 : rank * 512 + 512] = (
                        jnp.concatenate(parts, axis=0).astype(BF16)
                    )
                    return carry

                lax.fori_loop(0, PIX // 16, rows, 0)
        cover_v[...] = jnp.broadcast_to(1.0 / total, (8, 128))

    saves = [
        pltpu.make_async_copy(src, dst, out_sem.at[n])
        for n, (src, dst) in enumerate(
            ((roww, roww_h), (colt, colw_h), (cover_v, cover_h), (out_b, bal_h))
        )
    ]
    for sweep in range(SWEEPS):
        order = (1, 2) if sweep % 2 == 0 else (2, 1)
        disparity(0, sweep)
        if sweep == 0:
            loads[5].wait()
            take_coupling()
        elif sweep == 1:
            far_wait(1)
            far_signal(2)
            loads[9].wait()
            loads[10].wait()
            weights(0, roww)
            saves[0].start()
        else:
            weights(1, colw)
            colt[...] = colw[...].T
            saves[1].start()
            saves[2].start()
        for step, part in enumerate(order):
            take_responses(sweep, part - 1)
            if step == 0 and sweep < 2:
                far_wait(2 * sweep)
                far_signal(2 * sweep + 1)
            disparity(part, sweep)
        if sweep == 0:
            loads[6].wait()
            loads[7].wait()
            take_cross()
            loads[8].wait()
        solve(0, sweep)
        if sweep == 1:
            send_table()
        elif sweep == 2:
            far_wait(3)
        for part in order:
            take_grids(sweep, part - 1)
            solve(part, sweep)
    saves[3].start()

    lane8 = iota((8, 128), 1)
    lane_band = (lane8 % 64) // 16

    def fill(t):
        for rank in range(2):
            granule = tab_s[t, rank * 5]
            row = tab_s[t, rank * 5 + 1]
            halves = []
            for c in range(2):
                value = None
                for b in range(BD_):
                    x = out_b[granule, b, pl.ds(row + c, 8, stride=2), :]
                    x = pltpu.roll(x, tab_s[t, rank * 5 + 2 + b], axis=1)
                    value = x if value is None else jnp.where(lane_band == b, x, value)
                halves.append(value)
            pay_out[t, rank * 16 : rank * 16 + 16, :] = jnp.concatenate(halves, axis=0).astype(BF16)

    def pay_copy(k):
        return pltpu.make_async_remote_copy(
            src_ref=pay_out.at[lax.rem(me + k, NG)],
            dst_ref=pay_in.at[me],
            send_sem=as_sem.at[k],
            recv_sem=ar_sem.at[k],
            device_id=(lax.rem(me + k, NG), mb),
            device_id_type=MESH,
        )

    def fill_and_send(n, carry):
        steps = [lax.rem(12 + n * 4 + u, NG) for u in range(4)]
        for k in steps:
            fill(lax.rem(me + k, NG))
        for k in steps:

            @pl.when(k > 0)
            def _(k=k):
                pay_copy(k).start()

        return carry

    pltpu.make_async_copy(tab_v, tab_s, tab_sem).wait()
    lax.fori_loop(0, NG // 4, fill_and_send, 0)
    own_copy = pltpu.make_async_copy(pay_out.at[me], pay_in.at[me], own_sem)
    own_copy.start()
    own_copy.wait()
    for sweep in range(SWEEPS):
        for side in range(2):
            for piece in range(REACH + 1):
                halo_copy(sweep, side, piece).wait_send()
        for part in range(3):
            for k in range(1, NB):
                part_copy(sweep, part, k).wait_send()
    for save in saves:
        save.wait()

    def take_pay(k, carry):
        pltpu.make_async_remote_copy(
            src_ref=pay_out.at[lax.rem(me + k, NG)],
            dst_ref=pay_in.at[lax.rem(me + NG - k, NG)],
            send_sem=as_sem.at[k],
            recv_sem=ar_sem.at[k],
            device_id=(lax.rem(me + k, NG), mb),
            device_id_type=MESH,
        ).wait_recv()
        return carry

    lax.fori_loop(1, NG, take_pay, 0)

    def sent_pay(k, carry):
        pay_copy(k).wait_send()
        return carry

    lax.fori_loop(1, NG, sent_pay, 0)


def tile_kernel(
    pay_h,
    roww_h,
    colw_h,
    cover_h,
    pix_h,
    mid_h,
    bal_h,
    tile_h,
    pay_in,
    roww,
    colw,
    cover,
    pix_b,
    bal_b,
    tile_b,
    diagonal,
    rowpass,
    in_sem,
    out_sem,
):
    quarter = [pl.ds(4 * n, 4) for n in range(4)]
    pairs = [
        (pay_h, pay_in),
        (roww_h, roww),
        (colw_h, colw),
        (cover_h, cover),
        (pix_h, pix_b),
    ] + [(mid_h.at[part], bal_b.at[part]) for part in quarter]
    loads = [
        pltpu.make_async_copy(src, dst, in_sem.at[n]) for n, (src, dst) in enumerate(pairs)
    ]
    for load in loads:
        load.start()
    saves = [
        pltpu.make_async_copy(bal_b.at[part], bal_h.at[part], out_sem.at[n])
        for n, part in enumerate(quarter)
    ]

    def clear(n, carry):
        diagonal[n] = jnp.zeros((256, 256), BF16)
        return carry

    lax.fori_loop(0, 24, clear, 0)
    lane8 = iota((8, 128), 1)
    loads[0].wait()

    def expand(b):
        for group in range(4):
            rank, base = group // 2, (group % 2) * 16
            for s in range(16):
                block = pay_in[base + s, rank * 16 : rank * 16 + 16, :].astype(F32)
                for c in range(2):
                    parts = []
                    for parity in range(2):
                        turn = ((s % 8) * 16 - parity * 64 - b * 16) % 128
                        y = block[c * 8 : c * 8 + 8]
                        y = pltpu.roll(y, turn, axis=1) if turn else y
                        parts.append(jnp.where(lane8 // 16 == s % 8, y, 0.0))
                    diagonal[
                        group * 6 + b * 2 + c,
                        s * 16 : s * 16 + 16,
                        (s // 8) * 128 : (s // 8) * 128 + 128,
                    ] = jnp.concatenate(parts, axis=0).astype(BF16)

    expand(0)
    for load in loads[1:4]:
        load.wait()
    for load, save in zip(loads[5:], saves):
        load.wait()
        save.start()
    loads[4].wait()
    inverse_cover = cover[0:1, 0:1]

    for b in range(BD_):
        if b + 1 < BD_:
            expand(b + 1)
        fields = []
        for c in range(2):
            for group in range(4):
                cols = slice(group * 256, group * 256 + 256)
                rowpass[:, cols] = dot(roww[:, cols], diagonal[group * 6 + b * 2 + c]).astype(BF16)
            fields.append(dot(rowpass[...], colw[...]))
        pixels = pix_b[b].astype(F32)
        value = pixels * (1.0 + fields[0] * inverse_cover) + fields[1] * inverse_cover
        tile_b[b] = value.astype(BF16)
        pltpu.make_async_copy(tile_b.at[b], tile_h.at[b], out_sem.at[4 + b]).start()

    for save in saves:
        save.wait()
    for b in range(BD_):
        pltpu.make_async_copy(tile_b.at[b], tile_h.at[b], out_sem.at[4 + b]).wait()


def per_device(
    prior_grids,
    pif_rhs,
    pif_diagonal,
    pif_cross,
    pif_coupling,
    neighbour_offset,
    neighbour_count,
    tile_route,
    tile_window,
    tile_pixels,
):
    def pairs(x):
        return x.reshape(GD, BD_, 2, 32, 128).transpose(0, 1, 3, 2, 4).reshape(GD, BD_, 64, 128)

    prior = pairs(prior_grids)
    rhs = pairs(pif_rhs)
    diag = pairs(pif_diagonal)
    cross = (
        pif_cross.reshape(2, 8, BD_, 32, 128).transpose(2, 0, 3, 1, 4).reshape(BD_, 2, 256, 128)
    )
    coupling = (
        pif_coupling.reshape(GD, SLOTS, BD_, 32, 128)
        .transpose(0, 2, 3, 1, 4)
        .reshape(GD, BD_, 256, 128)
    )
    any_ = pl.BlockSpec(memory_space=pl.ANY)
    hbm = pl.BlockSpec(memory_space=pltpu.HBM)
    dma = pltpu.SemaphoreType.DMA
    middle, payload, roww, colw, cover = pl.pallas_call(
        kernel,
        out_shape=(
            jax.ShapeDtypeStruct((GD, BD_, 64, 128), F32),
            jax.ShapeDtypeStruct((NG, 32, 128), BF16),
            jax.ShapeDtypeStruct((PIX, 1024), BF16),
            jax.ShapeDtypeStruct((1024, PIX), BF16),
            jax.ShapeDtypeStruct((8, 128), F32),
        ),
        in_specs=[hbm] * 9,
        out_specs=(any_,) * 5,
        scratch_shapes=[
            pltpu.SMEM((SLOTS, GD), I32),
            pltpu.SMEM((GD,), I32),
            pltpu.VMEM((2, NG * GD), I32),
            pltpu.VMEM((2, 2, NG * GD), I32),
            pltpu.VMEM((GD, BD_, 64, 128), F32),
            pltpu.VMEM((GD, BD_, 64, 128), F32),
            pltpu.VMEM((GD, BD_, 64, 128), F32),
            pltpu.VMEM((BD_, 2, 256, 128), F32),
            pltpu.VMEM((GD, BD_, 256, 128), BF16),
            pltpu.VMEM((GD, BD_, 64, 128), F32),
            pltpu.VMEM((2, GD + 2 * REACH, BD_, 2, 4, 8, 128), F32),
            pltpu.VMEM((GD + 2 * REACH, BD_, 4, 8, 128), F32),
            pltpu.VMEM((GD, BD_, SLOTS, 4, 8, 128), F32),
            pltpu.VMEM((GD, BD_, 4, 8, 128), F32),
            pltpu.VMEM((512, 128), F32),
            pltpu.VMEM((512, 128), F32),
            pltpu.VMEM((3, 32, 128), F32),
            pltpu.VMEM((SWEEPS, 2, 2, REACH, BD_, 32, 128), BF16),
            pltpu.VMEM((SWEEPS, 2, 2, REACH, BD_, 32, 128), BF16),
            pltpu.VMEM((SWEEPS, 3, 32, 128), BF16),
            pltpu.VMEM((SWEEPS, 3, NB - 1, 32, 128), BF16),
            pltpu.VMEM((NG, 128), I32),
            pltpu.SMEM((NG, 128), I32),
            pltpu.VMEM((NG, 32, 128), BF16),
            pltpu.VMEM((PIX, 1024), BF16),
            pltpu.VMEM((PIX, 1024), BF16),
            pltpu.VMEM((1024, PIX), BF16),
            pltpu.VMEM((8, 128), F32),
            dma((11,)),
            dma((4,)),
            dma((SWEEPS, 2, REACH + 1)),
            dma((SWEEPS, 2, REACH + 1)),
            dma((SWEEPS, 3, NB - 1)),
            dma((SWEEPS, 3, NB - 1)),
            dma((NG,)),
            dma((NG,)),
            dma,
            dma,
            pltpu.SemaphoreType.REGULAR((FAR_STEPS, 2)),
        ],
        compiler_params=pltpu.CompilerParams(
            collective_id=0, has_side_effects=True, vmem_limit_bytes=36 * 1024 * 1024
        ),
        name="balance",
    )(
        *(
            pltpu.with_memory_space_constraint(x, pltpu.HBM)
            for x in (
                neighbour_offset.T,
                neighbour_count,
                prior,
                rhs,
                diag,
                cross,
                coupling,
                tile_route.T,
                tile_window.transpose(1, 2, 0),
            )
        )
    )
    balanced, tiles = pl.pallas_call(
        tile_kernel,
        out_shape=(
            jax.ShapeDtypeStruct((GD, BD_, 64, 128), F32),
            jax.ShapeDtypeStruct((BD_, PIX, PIX), BF16),
        ),
        in_specs=[any_] * 6,
        out_specs=(any_, any_),
        scratch_shapes=[
            pltpu.VMEM((NG, 32, 128), BF16),
            pltpu.VMEM((PIX, 1024), BF16),
            pltpu.VMEM((1024, PIX), BF16),
            pltpu.VMEM((8, 128), F32),
            pltpu.VMEM((BD_, PIX, PIX), BF16),
            pltpu.VMEM((GD, BD_, 64, 128), F32),
            pltpu.VMEM((BD_, PIX, PIX), BF16),
            pltpu.VMEM((24, 256, 256), BF16),
            pltpu.VMEM((PIX, 1024), BF16),
            dma((9,)),
            dma((7,)),
        ],
        compiler_params=pltpu.CompilerParams(vmem_limit_bytes=TILE_VMEM),
        name="tiles",
    )(payload, roww, colw, cover, tile_pixels[0], middle)
    balanced = (
        balanced.reshape(GD, BD_, 32, 2, 128)
        .transpose(0, 1, 3, 2, 4)
        .reshape(GD, BD_, 2, 4096)
    )
    return (balanced, tiles[None])


def solution(mesh):
    placed = (
        P("gran", "band", None, None),
        P("gran", "band", None, None),
        P("gran", "band", None, None),
        P("gran", "band", None),
        P("gran", None, "band", None),
        P("gran", None),
        P("gran"),
        P(),
        P(),
        P("gran", "band", None, None),
    )
    return jax.shard_map(
        per_device,
        mesh=mesh,
        in_specs=placed,
        out_specs=(P("gran", "band", None, None), P("gran", "band", None, None)),
        check_vma=False,
    )
```
